32 devices in a mesh: order: 4 (over x, core), blk: 8 (over z, y).
Axes of the slice: x: 2, y: 2, z: 4, core: 2. Of those that a mesh axis runs over, the one named last changes fastest.
Arguments:
- emode_coeffs: bfloat16 [4096, 16, 128], P('blk', 'order'), may hold values from -6 to 6
- lensing_coeffs: bfloat16 [4096, 16, 128], P('blk', 'order'), may hold values from -6 to 6
- order_values: int32 [16], replicated, may hold values from 0 to 4095, as said below
- circle_indices: int32 [1024], replicated, may hold values from 0 to 1023, each once
- circle_weights: float32 [1024], replicated, may hold values from 0.25 to 1
Outputs:
- gradient_part: bfloat16 [4096, 16, 128], P('blk', 'order')
- curl_part: bfloat16 [4096, 16, 128], P('blk', 'order')
The draws below stay inside these ranges and needn't reach their ends.
Inputs may be any that keep to these rules, and one draw needn't show every extreme that they name: `order_values`: distinct; exactly one value lies in each band from b * 256 to (b + 1) * 256 - 1. `circle_indices`: each circle of the sky exactly once.
All inputs are finite; a program needn't handle non-finite values.
Results may differ from the reference program's by a relative error of at most 0.012.
The reference program's roundings to bfloat16 on the way count: a program that leaves them out, or rounds other values in their place, can miss the bound.
Values may be sent and summed in bfloat16 or wider, within the bound.
A program may use at most 128 MiB of HBM per device.

```python
import math
import jax
import jax.numpy as jnp
from jax import lax

LMAX = 4096
ORDERS = 16
CIRCLE_DEV = 128
CIRCLES = 1024
SIMS = 64
LONGS = 256


def draw_order_values(key, part):
    stride = LMAX // ORDERS
    band_index = jax.random.permutation(jax.random.fold_in(key, 11), ORDERS).astype(jnp.int32)
    within = jax.random.randint(jax.random.fold_in(key, 12), (ORDERS,), 0, stride).astype(jnp.int32)
    within = jnp.where(band_index == 0, 0, within)
    within = jnp.where(band_index == ORDERS - 1, stride - 1, within)
    return (band_index * stride + within).astype(jnp.int32)


def steps_of(stream_key, extent, cuts, low, top_value):
    loudness, own = 1.0, jax.random.fold_in(stream_key, 6)
    for axis_at, blocks in cuts:
        heights = jnp.exp(jax.random.uniform(jax.random.fold_in(own, axis_at), (blocks,), jnp.float32, low / len(cuts), top_value / len(cuts)))
        loudness = loudness * jnp.repeat(heights, extent[axis_at] // blocks).reshape([-1 if axis == axis_at else 1 for axis in range(len(extent))])
    return loudness


def gaussian(rng, dims, scale, bound, shards=(), held_as=jnp.bfloat16):
    values = scale * jax.random.normal(rng, dims, jnp.float32)
    if shards:
        values = values * steps_of(rng, dims, shards, -0.22, 0.18)
    return jnp.clip(values, -bound, bound).astype(held_as)


def setup_inputs(seed: int = 0) -> dict:
    keys = jax.random.split(jax.random.key(seed), 6)
    emode_coeffs = gaussian(keys[0], (LMAX, ORDERS, 2 * SIMS), 1.0, 6.0, ((0, 8), (1, 4)))
    lensing_coeffs = gaussian(keys[1], (LMAX, ORDERS, 2 * SIMS), 1.0, 6.0, ((0, 8), (1, 4)))
    order_values = draw_order_values(jax.random.fold_in(keys[5], 71), 0)
    circle_indices = jax.random.permutation(keys[3], CIRCLES).astype(jnp.int32)
    circle_weights = jnp.clip(jnp.exp(jax.random.uniform(keys[4], (CIRCLES,), jnp.float32, math.log(0.25), math.log(1.0))), 0.25, 1.0)
    return {"emode_coeffs": emode_coeffs, "lensing_coeffs": lensing_coeffs, "order_values": order_values, "circle_indices": circle_indices, "circle_weights": circle_weights}


def spin_tables(degrees, circle_list, order_list, spin_shift, circle_total):
    frequency = 2 * degrees + 1 + spin_shift
    colatitude = 2 * circle_list + 1
    phases = colatitude[None, :, None] * frequency[None, None, :] - 2 * circle_total * order_list[:, None, None]
    phases = jnp.mod(phases, 8 * circle_total)
    angles = phases.astype(jnp.float32) * (math.pi / (4 * circle_total))
    amplitude = math.sqrt(2.0 / LMAX)
    inside = degrees[None, None, :] >= order_list[:, None, None]
    cosine = jnp.where(inside, amplitude * jnp.cos(angles), 0.0)
    weight_deg = (frequency.astype(jnp.float32) / (2.0 * LMAX))[None, None, :]
    slopes = jnp.where(inside, -weight_deg * amplitude * jnp.sin(angles), 0.0)
    return (cosine.astype(jnp.bfloat16), slopes.astype(jnp.bfloat16))

def longitude_table(circle_list, order_list):
    full_circle = 2 * LMAX
    longitude = jnp.arange(LONGS, dtype=jnp.int32)
    parity = jnp.mod(circle_list, 2)
    phase_steps = order_list[None, :, None] * (2 * longitude[None, None, :] + parity[:, None, None])
    phase_steps = jnp.mod(phase_steps, 2 * full_circle)
    angles = phase_steps.astype(jnp.float32) * (math.pi / full_circle)
    scaling = 1.0 / math.sqrt(order_list.shape[0])
    fourier = jnp.concatenate([jnp.cos(angles) * scaling, -jnp.sin(angles) * scaling], axis=1)
    return fourier.astype(jnp.bfloat16)

def rotate(block, factor):
    return jnp.concatenate([-block[..., SIMS:], block[..., :SIMS]], axis=-1) * factor

def reference(emode_coeffs, lensing_coeffs, order_values, circle_indices, circle_weights):
    csims = 2 * SIMS
    degrees = jnp.arange(LMAX, dtype=jnp.int32)

    def synth_order(order_slot):
        order_one = lax.dynamic_slice_in_dim(order_values, order_slot, 1)
        emode = lax.dynamic_index_in_dim(emode_coeffs, order_slot, 1, keepdims=False)
        lens = lax.dynamic_index_in_dim(lensing_coeffs, order_slot, 1, keepdims=False)
        cos_plus, der_plus = spin_tables(degrees, circle_indices, order_one, 2, CIRCLES)
        cos_minus, der_minus = spin_tables(degrees, circle_indices, order_one, -2, CIRCLES)
        cos_zero, der_zero = spin_tables(degrees, circle_indices, order_one, 0, CIRCLES)
        factor = order_one[0].astype(jnp.float32) / LMAX
        q_theta = jnp.dot(der_plus[0], emode, preferred_element_type=jnp.float32)
        u_theta = jnp.dot(der_minus[0], emode, preferred_element_type=jnp.float32)
        q_cos = jnp.dot(cos_plus[0], emode, preferred_element_type=jnp.float32)
        u_cos = jnp.dot(cos_minus[0], emode, preferred_element_type=jnp.float32)
        d_theta = jnp.dot(der_zero[0], lens, preferred_element_type=jnp.float32)
        d_cos = jnp.dot(cos_zero[0], lens, preferred_element_type=jnp.float32)
        joined = jnp.concatenate([q_theta, u_theta, rotate(q_cos, factor), rotate(u_cos, factor), d_theta, rotate(d_cos, factor)], axis=-1)
        return joined.astype(jnp.bfloat16)
    modes = lax.map(synth_order, jnp.arange(ORDERS, dtype=jnp.int32))
    nblocks = CIRCLES // CIRCLE_DEV
    mode_blocks = modes.reshape(ORDERS, nblocks, CIRCLE_DEV, 6 * csims).transpose(1, 0, 2, 3)
    circle_blocks = circle_indices.reshape(nblocks, CIRCLE_DEV)
    weight_blocks = circle_weights.reshape(nblocks, CIRCLE_DEV)

    def pixel_block(operands):
        block_modes, block_circles, block_weights = operands
        arranged = block_modes.reshape(ORDERS, CIRCLE_DEV, 6, 2, SIMS).transpose(1, 3, 0, 2, 4)
        arranged = arranged.reshape(CIRCLE_DEV, 2 * ORDERS, 6 * SIMS)
        fourier = longitude_table(block_circles, order_values)
        pixels = jnp.einsum('knj,knc->kjc', fourier.astype(jnp.float32), arranged.astype(jnp.float32))
        pixels = pixels.reshape(CIRCLE_DEV, LONGS, 6, SIMS)
        delta_q = pixels[:, :, 4] * pixels[:, :, 0] + pixels[:, :, 5] * pixels[:, :, 2]
        delta_u = pixels[:, :, 4] * pixels[:, :, 1] + pixels[:, :, 5] * pixels[:, :, 3]
        deflected = jnp.concatenate([delta_q, delta_u], axis=-1).astype(jnp.bfloat16)
        analysed = jnp.einsum('knj,kjc->knc', fourier.astype(jnp.float32), deflected.astype(jnp.float32))
        weighted = (analysed * block_weights[:, None, None]).astype(jnp.bfloat16)
        weighted = weighted.reshape(CIRCLE_DEV, 2, ORDERS, 2, SIMS).transpose(0, 2, 3, 1, 4)
        return weighted.reshape(CIRCLE_DEV, ORDERS, 4 * SIMS)
    weighted_all = lax.map(pixel_block, (mode_blocks, circle_blocks, weight_blocks))
    weighted_all = weighted_all.reshape(CIRCLES, ORDERS, 4 * SIMS)

    def adjoint_order(order_slot):
        order_one = lax.dynamic_slice_in_dim(order_values, order_slot, 1)
        circle_maps = lax.dynamic_index_in_dim(weighted_all, order_slot, 1, keepdims=False)
        cos_plus, unused_plus = spin_tables(degrees, circle_indices, order_one, 2, CIRCLES)
        cos_minus, unused_minus = spin_tables(degrees, circle_indices, order_one, -2, CIRCLES)
        plus = jnp.dot(cos_plus[0].T, circle_maps, preferred_element_type=jnp.float32)
        minus = jnp.dot(cos_minus[0].T, circle_maps, preferred_element_type=jnp.float32)
        gradient = plus[:, :csims] + minus[:, csims:]
        curl = plus[:, csims:] - minus[:, :csims]
        return jnp.concatenate([gradient, curl], axis=-1)
    summed = lax.map(adjoint_order, jnp.arange(ORDERS, dtype=jnp.int32)).transpose(1, 0, 2)
    return (summed[..., :csims].astype(jnp.bfloat16), summed[..., csims:].astype(jnp.bfloat16))
```

```python
import functools
import math

import jax
import jax.numpy as jnp
from jax import lax
from jax.experimental import pallas as pl
from jax.experimental.pallas import tpu as pltpu
from jax.sharding import PartitionSpec as P

LONGS = 256
BF = jnp.bfloat16
F32 = jnp.float32
MESH = pl.DeviceIdType.MESH


def wrap(value, period):
    if period & (period - 1) == 0:
        return value & (period - 1)
    return jnp.mod(value, period)


def sin_cos(steps, period):
    quarter = period // 4
    steps = wrap(steps, period)
    turn = (steps + quarter // 2) // quarter if quarter & (quarter - 1) else (steps + quarter // 2) >> (quarter.bit_length() - 1)
    x = (steps - turn * quarter).astype(F32) * (2.0 * math.pi / period)
    x2 = x * x
    s = x * (1.0 + x2 * (-1.0 / 6 + x2 * (1.0 / 120 + x2 * (-1.0 / 5040 + x2 * (1.0 / 362880)))))
    c = 1.0 + x2 * (-0.5 + x2 * (1.0 / 24 + x2 * (-1.0 / 720 + x2 * (1.0 / 40320))))
    odd = (turn & 1) == 1
    sine = jnp.where(odd, c, s)
    cosine = jnp.where(odd, s, c)
    sine = jnp.where((turn & 2) == 2, -sine, sine)
    cosine = jnp.where(((turn + 1) & 2) == 2, -cosine, cosine)
    return sine, cosine


def quarter_turns(order):
    turn = order & 3
    c = jnp.where(turn == 0, 1.0, jnp.where(turn == 2, -1.0, 0.0)).astype(F32)
    s = jnp.where(turn == 1, 1.0, jnp.where(turn == 3, -1.0, 0.0)).astype(F32)
    return c, s


def neighbours(order_size, line):
    order_pos, blk = lax.axis_index("order"), lax.axis_index("blk")
    h, y = lax.div(blk, 2), lax.rem(blk, 2)
    pair = blk + 1 - 2 * y
    peers = [lax.rem(order_pos + k, order_size) for k in range(1, order_size)]
    return order_pos, blk, h, y, pair, peers


def greet(order_size, line):
    order_pos, blk, h, y, pair, peers = neighbours(order_size, line)
    barrier = pltpu.get_barrier_semaphore()

    @pl.when(h > 0)
    def _():
        pl.semaphore_signal(barrier, inc=1, device_id={"blk": blk - 2}, device_id_type=MESH)

    @pl.when(h < line - 1)
    def _():
        pl.semaphore_signal(barrier, inc=1, device_id={"blk": blk + 2}, device_id_type=MESH)

    pl.semaphore_signal(barrier, inc=1, device_id={"blk": pair}, device_id_type=MESH)
    for peer in peers:
        pl.semaphore_signal(barrier, inc=1, device_id={"order": peer}, device_id_type=MESH)
    ends = jnp.where(h > 0, 1, 0) + jnp.where(h < line - 1, 1, 0)
    pl.semaphore_wait(barrier, order_size + ends)


def remote(src, dst, send, recv, device):
    return pltpu.make_async_remote_copy(
        src_ref=src, dst_ref=dst, send_sem=send, recv_sem=recv, device_id=device, device_id_type=MESH
    )


def synth_kernel(
    lmax, circle_total, line, order_size, orders, csims,
    m_ref, r_ref, line_ref, e_ref, p_ref, out_ref,
    held, land, tab, acc, own, ysend, yrecv, asend, lens, ltab, lpart, csend, crecv,
    zs, zr, ys, yr, as_, ar, ls, lr, cs, cr,
):
    order_pos, blk, h, y, pair, peers = neighbours(order_size, line)
    rows = e_ref.shape[1]
    circles = r_ref.shape[0] // 2
    part = circles // order_size
    amplitude = math.sqrt(2.0 / lmax)
    colat = 2 * r_ref[...] + 1

    def along(src, block, o, way):
        return remote(
            src, held.at[block, o], zs.at[way, block, o], zr.at[block, o], {"blk": blk - 2 + 4 * way}
        )

    def send_own(o):
        @pl.when(h > 0)
        def _():
            along(e_ref.at[o], h, o, 0).start()

        @pl.when(h < line - 1)
        def _():
            along(e_ref.at[o], h, o, 1).start()

    def across(o):
        return remote(ysend.at[o], yrecv.at[o], ys.at[o], yr.at[o], {"blk": pair})

    def spread(o, peer, source):
        begin = pl.multiple_of(peer * part, part)
        return remote(
            asend.at[o, pl.ds(begin, part)], land.at[source * orders + o],
            as_.at[peer, o], ar.at[source, o], {"order": peer},
        )

    def share(o, lane):
        begin = pl.multiple_of(lane * rows, rows)
        return remote(
            p_ref.at[o], lens.at[o, pl.ds(begin, rows)], ls.at[o], lr.at[o], {"blk": pair}
        )

    def chain(way, target, o):
        return remote(
            csend.at[way, target, o], crecv.at[way, target, o],
            cs.at[way, target, o], cr.at[way, target, o], {"blk": blk - 2 + 4 * way},
        )

    greet(order_size, line)
    for o in range(orders):
        share(o, y).start()
        send_own(o)
    lens[:, pl.ds(pl.multiple_of(y * rows, rows), rows), :] = p_ref[...]

    def make_table(block, carry):
        degree = (2 * block + y) * rows + lax.broadcasted_iota(jnp.int32, (1, rows), 1)
        freq = 2 * degree + 1
        sine, cosine = sin_cos(colat * freq, 8 * circle_total)
        sine, cosine = sine * amplitude, cosine * amplitude
        weight = freq.astype(F32) / (2.0 * lmax)
        for k, value in enumerate((cosine, sine, cosine * weight, sine * weight)):
            tab[block, 2 * k * circles : 2 * (k + 1) * circles, :] = value.astype(BF)
        return carry

    def make_lens_table(target, carry):
        degree = 2 * h * rows + lax.broadcasted_iota(jnp.int32, (1, 2 * rows), 1)
        freq = 2 * degree + 1
        sine, cosine = sin_cos((2 * line_ref[target] + 1) * freq, 8 * circle_total)
        sine, cosine = sine * amplitude, cosine * amplitude
        weight = freq.astype(F32) / (2.0 * lmax)
        for k, value in enumerate((cosine, sine, sine * weight, cosine * weight)):
            ltab[k, target] = value.astype(BF)
        return carry

    lax.fori_loop(0, line, make_lens_table, 0)
    lax.fori_loop(0, line, make_table, 0)
    ps, pc = sin_cos(colat * 2, 8 * circle_total)
    kappa = 2.0 / (2.0 * lmax)

    def product(values, block, o):
        degree = (2 * block + y) * rows + lax.broadcasted_iota(jnp.int32, values.shape, 0)
        values = jnp.where(degree >= m_ref[o], values, jnp.zeros_like(values))
        return jnp.dot(tab[block], values, preferred_element_type=F32)

    def finish(o):
        across(o).wait_recv()
        cut = 4 * csims
        asend[o, :, :cut] = (own[o] + yrecv[o].astype(F32)).astype(BF)
        asend[o, :, cut:] = lpart[o, h].astype(BF)
        for peer in peers:
            spread(o, peer, order_pos).start()
        begin = pl.multiple_of(order_pos * part, part)
        land[order_pos * orders + o] = asend[o, pl.ds(begin, part)]

    def lens_sums(o):
        share(o, 1 - y).wait_recv()
        m = m_ref[o]
        cm, sm = quarter_turns(m)
        values = lens[o]
        degree = 2 * h * rows + lax.broadcasted_iota(jnp.int32, values.shape, 0)
        values = jnp.where(degree >= m, values, jnp.zeros_like(values))
        flat, split = (line * circles, 2 * rows), (line, circles, csims)
        theta = jnp.dot(ltab[2 + (m & 1)].reshape(flat), values, preferred_element_type=F32)
        lpart[o, :, :, :csims] = ((sm - cm) * theta).reshape(split)
        flow = jnp.dot(ltab[m & 1].reshape(flat), values, preferred_element_type=F32)
        lpart[o, :, :, csims:] = ((cm + sm) * (m.astype(F32) * (1.0 / lmax)) * flow).reshape(split)

    def stage(t, o):
        def leftward(target, carry):
            @pl.when((target <= h) & (h < line - 1))
            def _():
                chain(0, target, o).wait_recv()
                lpart[o, target] += crecv[0, target, o].astype(F32)

            @pl.when(target < h)
            def _():
                csend[0, target, o] = lpart[o, target].astype(BF)
                chain(0, target, o).start()

            return carry

        def rightward(target, carry):
            @pl.when((target >= h) & (h > 0))
            def _():
                chain(1, target, o).wait_recv()
                lpart[o, target] += crecv[1, target, o].astype(F32)

            @pl.when(target > h)
            def _():
                csend[1, target, o] = lpart[o, target].astype(BF)
                chain(1, target, o).start()

            return carry

        @pl.when(h == line - 1 - t)
        def _():
            lax.fori_loop(0, line, leftward, 0)

        @pl.when(h == t)
        def _():
            lax.fori_loop(0, line, rightward, 0)

    def hop(s, o):
        after, before = h + s, h - s

        @pl.when(after < line)
        def _():
            along(held.at[after, o], after, o, 0).wait_recv()

            @pl.when(h > 0)
            def _():
                along(held.at[after, o], after, o, 0).start()

        @pl.when(before >= 0)
        def _():
            along(held.at[before, o], before, o, 1).wait_recv()

            @pl.when(h < line - 1)
            def _():
                along(held.at[before, o], before, o, 1).start()

        @pl.when(after < line)
        def _():
            acc[o] += product(held[after, o], after, o)

        @pl.when(before >= 0)
        def _():
            acc[o] += product(held[before, o], before, o)

    def emode_maps(o):
        cm, sm = quarter_turns(m_ref[o])
        factor = m_ref[o].astype(F32) * (1.0 / lmax)
        c0, s0, gc0, gs0 = (acc[o, 2 * k * circles : 2 * (k + 1) * circles] for k in range(4))
        a, b = cm * c0 + sm * s0, cm * s0 - sm * c0
        gc, gs = cm * gc0 + sm * gs0, cm * gs0 - sm * gc0
        maps = (
            -(pc * (gs + kappa * b) + ps * (gc + kappa * a)),
            -(pc * (gs - kappa * b) - ps * (gc - kappa * a)),
            factor * (pc * a - ps * b),
            factor * (pc * a + ps * b),
        )
        for k, value in enumerate(maps):
            at = slice(k * csims, (k + 1) * csims)
            own[o, :, at] = value[:circles]
            ysend[o, :, at] = value[circles:].astype(BF)
        across(o).start()

    def one_phase(s, outer):
        def one_order(o, carry):
            @pl.when(s < line)
            def _():
                hop(s, o)

            @pl.when(s == 1)
            def _():
                lens_sums(o)

            @pl.when(s == line - 1)
            def _():
                emode_maps(o)

            stage(s - 1, o)

            @pl.when(s == line)
            def _():
                finish(o)

            return carry

        return lax.fori_loop(0, orders, one_order, outer)

    def own_product(o, carry):
        acc[o] = product(e_ref[o], h, o)
        return carry

    lax.fori_loop(0, orders, own_product, 0)
    lax.fori_loop(1, line + 1, one_phase, 0)

    def settle(o, carry):
        across(o).wait_send()
        share(o, y).wait_send()
        for peer in peers:
            spread(o, peer, order_pos).wait_send()
            spread(o, peer, peer).wait_recv()

        def sent(block, inner):
            @pl.when((h > 0) & (block >= h))
            def _():
                along(held.at[block, o], block, o, 0).wait_send()

            @pl.when((h < line - 1) & (block <= h))
            def _():
                along(held.at[block, o], block, o, 1).wait_send()

            @pl.when(block < h)
            def _():
                chain(0, block, o).wait_send()

            @pl.when(block > h)
            def _():
                chain(1, block, o).wait_send()

            return inner

        lax.fori_loop(0, line, sent, 0)
        return carry

    lax.fori_loop(0, orders, settle, 0)
    out_ref[...] = land[...]


def pixel_kernel(orders, csims, par_ref, w_ref, m_ref, f_ref, ft_ref, out_ref):
    count = m_ref.shape[0]
    sims = csims // 2
    low = lax.broadcasted_iota(jnp.int32, (orders, csims), 1) < sims
    begin = pl.program_id(0) * count

    def halves(x, y):
        first = jnp.where(low, x, pltpu.roll(y, sims, 1))
        second = jnp.where(low, pltpu.roll(x, sims, 1), y)
        return first, second

    for c in range(count):
        qt, ut, qc, uc, dt, dc = (
            m_ref[c, :, k * csims : (k + 1) * csims].astype(F32) for k in range(6)
        )
        t_re, t_im = halves(qt, ut)
        c_re, c_im = halves(qc, uc)
        dt_re, dt_im = halves(dt, dt)
        dc_re, dc_im = halves(dc, dc)
        real = jnp.concatenate([t_re, -c_im, dt_re, -dc_im], axis=1)
        imag = jnp.concatenate([t_im, c_re, dt_im, dc_re], axis=1)
        arranged = jnp.concatenate([real, imag], axis=0).astype(BF)
        parity = par_ref[begin + c]
        pixels = jnp.dot(ft_ref[parity], arranged, preferred_element_type=F32)
        deflected = (
            pixels[:, 2 * csims : 3 * csims] * pixels[:, :csims]
            + pixels[:, 3 * csims :] * pixels[:, csims : 2 * csims]
        ).astype(BF)
        analysed = jnp.dot(f_ref[parity], deflected, preferred_element_type=F32) * w_ref[begin + c]
        gq, gu = halves(analysed[:orders], analysed[orders:])
        out_ref[c, :, :csims] = gq.astype(BF)
        out_ref[c, :, csims:] = gu.astype(BF)


def adjoint_kernel(
    lmax, circle_total, line, order_size, orders, csims,
    m_ref, r_ref, rc_ref, w_ref, grad_ref, curl_ref,
    gath, tab, acc, zs, zr, ys, yr, as_, ar,
):
    order_pos, blk, h, y, pair, peers = neighbours(order_size, line)
    degrees = grad_ref.shape[0]
    circles = gath.shape[2]
    part = w_ref.shape[1]
    amplitude = math.sqrt(2.0 / lmax)

    def back(peer, source):
        begin = pl.multiple_of(source * part, part)
        return remote(
            w_ref.at[pl.ds(peer * orders, orders)], gath.at[blk, :, pl.ds(begin, part)],
            as_.at[peer], ar.at[source], {"order": peer},
        )

    def along(line_at, way):
        block = gath.at[2 * line_at + y]
        return remote(block, block, zs.at[way, line_at], zr.at[line_at], {"blk": blk - 2 + 4 * way})

    def across(line_at, lane):
        block = gath.at[2 * line_at + lane]
        return remote(block, block, ys.at[line_at], yr.at[line_at], {"blk": pair})

    greet(order_size, line)
    for peer in peers:
        back(peer, order_pos).start()
    begin = pl.multiple_of(order_pos * part, part)
    gath[blk, :, pl.ds(begin, part), :] = w_ref[pl.ds(order_pos * orders, orders)]

    def make_table(block, carry):
        degree = blk * degrees + lax.broadcasted_iota(jnp.int32, (degrees, 1), 0)
        sine, cosine = sin_cos((2 * degree + 1) * (2 * r_ref[block] + 1), 8 * circle_total)
        tab[block, :, :circles] = (cosine * amplitude).astype(BF)
        tab[block, :, circles:] = (sine * amplitude).astype(BF)
        return carry

    lax.fori_loop(0, line // 2, make_table, 0)

    def add(block):
        ps, pc = sin_cos(2 * (2 * rc_ref[block] + 1), 8 * circle_total)
        ups, vps = [], []
        for o in range(orders):
            cm, sm = quarter_turns(m_ref[o])
            gq = gath[block, o, :, :csims].astype(F32)
            gu = gath[block, o, :, csims:].astype(F32)
            x1, y1 = pc * (gq + gu), ps * (gq - gu)
            x2, y2 = pc * (gu - gq), ps * (gu + gq)
            ups += [(cm * x1 + sm * y1).astype(BF), (cm * x2 + sm * y2).astype(BF)]
            vps += [(sm * x1 - cm * y1).astype(BF), (sm * x2 - cm * y2).astype(BF)]
        values = jnp.concatenate(
            [jnp.concatenate(ups, axis=1), jnp.concatenate(vps, axis=1)], axis=0
        )
        acc[...] += jnp.dot(tab[block], values, preferred_element_type=F32)

    for peer in peers:
        back(peer, peer).wait_recv()

    @pl.when(h > 0)
    def _():
        along(h, 0).start()

    @pl.when(h < line - 1)
    def _():
        along(h, 1).start()

    across(h, y).start()
    lax.fori_loop(line // 2, 2 * line, make_table, 0)
    acc[...] = jnp.zeros_like(acc)

    def hop(s, carry):
        after, before = h + s, h - s

        @pl.when((s > 0) & (after < line))
        def _():
            along(after, 0).wait_recv()

            @pl.when(h > 0)
            def _():
                along(after, 0).start()

            across(after, y).start()

        @pl.when((s > 0) & (before >= 0))
        def _():
            along(before, 1).wait_recv()

            @pl.when(h < line - 1)
            def _():
                along(before, 1).start()

            across(before, y).start()

        @pl.when(after < line)
        def _():
            add(2 * after + y)

        @pl.when((s > 0) & (before >= 0))
        def _():
            add(2 * before + y)

        return carry

    lax.fori_loop(0, line, hop, 0)

    def cross(s, carry):
        after, before = h + s, h - s

        @pl.when(after < line)
        def _():
            across(after, 1 - y).wait_recv()
            add(2 * after + 1 - y)

        @pl.when((s > 0) & (before >= 0))
        def _():
            across(before, 1 - y).wait_recv()
            add(2 * before + 1 - y)

        return carry

    lax.fori_loop(0, line, cross, 0)
    for peer in peers:
        back(peer, order_pos).wait_send()

    def settle(line_at, carry):
        across(line_at, y).wait_send()

        @pl.when((h > 0) & (line_at >= h))
        def _():
            along(line_at, 0).wait_send()

        @pl.when((h < line - 1) & (line_at <= h))
        def _():
            along(line_at, 1).wait_send()

        return carry

    lax.fori_loop(0, line, settle, 0)
    rows = blk * degrees + lax.broadcasted_iota(jnp.int32, (degrees, csims), 0)
    for o in range(orders):
        inside = rows >= m_ref[o]
        at = slice(o * csims, (o + 1) * csims)
        grad = acc[:, 2 * o * csims : (2 * o + 1) * csims]
        curl = acc[:, (2 * o + 1) * csims : (2 * o + 2) * csims]
        grad_ref[:, at] = jnp.where(inside, grad, 0.0).astype(BF)
        curl_ref[:, at] = jnp.where(inside, curl, 0.0).astype(BF)


def longitude_table(lmax, parity, order_list):
    full_circle = 2 * lmax
    longitude = jnp.arange(LONGS, dtype=jnp.int32)
    phase_steps = order_list[None, :, None] * (2 * longitude[None, None, :] + parity[:, None, None])
    phase_steps = jnp.mod(phase_steps, 2 * full_circle)
    angles = phase_steps.astype(jnp.float32) * (math.pi / full_circle)
    scaling = 1.0 / math.sqrt(order_list.shape[0])
    fourier = jnp.concatenate([jnp.cos(angles) * scaling, -jnp.sin(angles) * scaling], axis=1)
    return fourier.astype(BF)


def divisor(total, limit):
    return next(k for k in range(min(total, limit), 0, -1) if total % k == 0)


SMEM = pl.BlockSpec(memory_space=pltpu.SMEM)
VMEM = pl.BlockSpec(memory_space=pltpu.VMEM)
PARAMS = pltpu.CompilerParams(vmem_limit_bytes=48 << 20)


def by_circle(order_size, blk_size, emode_coeffs, lensing_coeffs, order_values, circle_indices, circle_weights):
    degree_local, orders, csims = emode_coeffs.shape
    lmax = degree_local * blk_size
    circle_total = circle_indices.shape[0]
    order_total = order_values.shape[0]
    circles = circle_total // blk_size
    order_pos = lax.axis_index("order")
    block_pos = lax.axis_index("blk")
    my_orders = lax.dynamic_slice_in_dim(order_values, order_pos * orders, orders)
    width = orders * csims
    line = blk_size // 2
    blocks = circle_indices.reshape(blk_size, circles)
    pair_circles = jnp.concatenate(
        [
            lax.dynamic_index_in_dim(blocks, block_pos, 0, keepdims=False),
            lax.dynamic_index_in_dim(blocks, block_pos ^ 1, 0, keepdims=False),
        ]
    )
    line_circles = lax.dynamic_index_in_dim(
        circle_indices.reshape(line, 2, circles), block_pos % 2, 1, keepdims=False
    )
    fourier = longitude_table(lmax, jnp.arange(2, dtype=jnp.int32), order_values)
    fourier_t = fourier.transpose(0, 2, 1)
    part = circles // order_size
    dma = pltpu.SemaphoreType.DMA
    spread = pl.pallas_call(
        functools.partial(synth_kernel, lmax, circle_total, line, order_size, orders, csims),
        out_shape=jax.ShapeDtypeStruct((order_total, part, 6 * csims), BF),
        in_specs=[SMEM, VMEM, VMEM, VMEM, VMEM],
        out_specs=VMEM,
        scratch_shapes=[
            pltpu.VMEM((line, orders, degree_local, csims), BF),
            pltpu.VMEM((order_total, part, 6 * csims), BF),
            pltpu.VMEM((line, 8 * circles, degree_local), BF),
            pltpu.VMEM((orders, 8 * circles, csims), F32),
            pltpu.VMEM((orders, circles, 4 * csims), F32),
            pltpu.VMEM((orders, circles, 4 * csims), BF),
            pltpu.VMEM((orders, circles, 4 * csims), BF),
            pltpu.VMEM((orders, circles, 6 * csims), BF),
            pltpu.VMEM((orders, 2 * degree_local, csims), BF),
            pltpu.VMEM((4, line, circles, 2 * degree_local), BF),
            pltpu.VMEM((orders, line, circles, 2 * csims), F32),
            pltpu.VMEM((2, line, orders, circles, 2 * csims), BF),
            pltpu.VMEM((2, line, orders, circles, 2 * csims), BF),
            dma((2, line, orders)),
            dma((line, orders)),
            dma((orders,)),
            dma((orders,)),
            dma((order_size, orders)),
            dma((order_size, orders)),
            dma((orders,)),
            dma((orders,)),
            dma((2, line, orders)),
            dma((2, line, orders)),
        ],
        compiler_params=pltpu.CompilerParams(
            vmem_limit_bytes=48 << 20, collective_id=0, has_side_effects=True
        ),
        name="synth",
    )(
        my_orders,
        pair_circles[:, None],
        line_circles[:, :, None],
        emode_coeffs.transpose(1, 0, 2),
        lensing_coeffs.transpose(1, 0, 2),
    )
    spread = spread.transpose(1, 0, 2)
    begin = block_pos * circles + order_pos * part
    part_circles = lax.dynamic_slice_in_dim(circle_indices, begin, part)
    part_weights = lax.dynamic_slice_in_dim(circle_weights, begin, part)
    count = divisor(part, 8)
    weighted = pl.pallas_call(
        functools.partial(pixel_kernel, order_total, csims),
        out_shape=jax.ShapeDtypeStruct((part, order_total, 2 * csims), BF),
        grid=(part // count,),
        in_specs=[
            SMEM,
            SMEM,
            pl.BlockSpec((count, order_total, 6 * csims), lambda i: (i, 0, 0)),
            pl.BlockSpec((2, 2 * order_total, LONGS), lambda i: (0, 0, 0)),
            pl.BlockSpec((2, LONGS, 2 * order_total), lambda i: (0, 0, 0)),
        ],
        out_specs=pl.BlockSpec((count, order_total, 2 * csims), lambda i: (i, 0, 0)),
        compiler_params=PARAMS,
        name="pixels",
    )(jnp.mod(part_circles, 2), part_weights, spread, fourier, fourier_t)
    grad, curl = pl.pallas_call(
        functools.partial(adjoint_kernel, lmax, circle_total, line, order_size, orders, csims),
        out_shape=[jax.ShapeDtypeStruct((degree_local, width), BF)] * 2,
        in_specs=[SMEM, VMEM, VMEM, VMEM],
        out_specs=[VMEM, VMEM],
        scratch_shapes=[
            pltpu.VMEM((blk_size, orders, circles, 2 * csims), BF),
            pltpu.VMEM((blk_size, degree_local, 2 * circles), BF),
            pltpu.VMEM((degree_local, 2 * width), F32),
            dma((2, line)),
            dma((line,)),
            dma((line,)),
            dma((line,)),
            dma((order_size,)),
            dma((order_size,)),
        ],
        compiler_params=pltpu.CompilerParams(
            vmem_limit_bytes=48 << 20, collective_id=1, has_side_effects=True
        ),
        name="adjoint",
    )(my_orders, blocks[:, None, :], blocks[:, :, None], weighted.transpose(1, 0, 2))
    return grad.reshape(emode_coeffs.shape), curl.reshape(emode_coeffs.shape)


def turned(dims, left, right):
    return lax.dot_general(left, right, (dims, ((), ())), preferred_element_type=F32)


def realization_kernel(
    lmax, circle_total, order_size, blk_size, orders, csims, group,
    em_ref, le_ref, m_ref, ci_ref, cw_ref, grad_ref, curl_ref,
    pick, out1, land1, out2, land2, tab, xs, maps, waves, waves_t, ana, pairs, wlane,
    s1, r1, s2, r2,
):
    order_pos, blk = lax.axis_index("order"), lax.axis_index("blk")
    devices = order_size * blk_size
    me = order_pos * blk_size + blk
    degrees = em_ref.shape[0]
    half = degrees // 2
    sims = csims // 2
    low = blk_size // 2
    span = low * half
    couples = circle_total // 2
    quarter = couples // 2
    rows = order_size * 2 * orders
    tile = 2 * orders
    full = 8 * circle_total
    width = orders * csims

    def peer(k):
        to_order = lax.rem(order_pos + (order_size - 1) - lax.rem(k, order_size), order_size)
        to_blk = lax.rem(blk + (blk_size - 1) - lax.div(k, order_size), blk_size)
        return to_order, to_blk

    def hand(src, dst, send, recv, s, k):
        o, b = peer(k)
        return pltpu.make_async_remote_copy(
            src_ref=src.at[s, o, b], dst_ref=dst.at[s, order_pos, blk],
            send_sem=send.at[s, o, b], recv_sem=recv.at[s, order_pos, blk],
            device_id={"order": o, "blk": b}, device_id_type=MESH,
        )

    def arrival(src, dst, send, recv, s, k):
        o, b = peer(k)
        return pltpu.make_async_remote_copy(
            src_ref=src.at[s, o, b], dst_ref=dst.at[s, o, b],
            send_sem=send.at[s, o, b], recv_sem=recv.at[s, o, b],
            device_id={"order": o, "blk": b}, device_id_type=MESH,
        )

    first = (out1, land1, s1, r1)
    second = (out2, land2, s2, r2)

    def send_all(args, s):
        def one(k, carry):
            hand(*args, s, k).start()
            return carry

        lax.fori_loop(0, devices - 1, one, 0)

    def await_all(args, s):
        def one(k, carry):
            arrival(*args, s, k).wait_recv()
            return carry

        lax.fori_loop(0, devices - 1, one, 0)

    def sent_all(args, s):
        def one(k, carry):
            hand(*args, s, k).wait_send()
            return carry

        lax.fori_loop(0, devices - 1, one, 0)

    barrier = pltpu.get_barrier_semaphore()

    def greet_one(k, carry):
        o, b = peer(k)
        pl.semaphore_signal(barrier, inc=1, device_id={"order": o, "blk": b}, device_id_type=MESH)
        return carry

    lax.fori_loop(0, devices - 1, greet_one, 0)

    def arrange(s):
        row = lax.broadcasted_iota(jnp.int32, (devices * tile, 1), 0)
        within = lax.rem(row, tile)
        column = (
            lax.rem(within, orders) * csims + lax.div(within, orders) * sims + lax.div(row, tile) * group + s
        )
        lane = lax.broadcasted_iota(jnp.int32, (devices * tile, width), 1)
        choice = jnp.where(lane == column, 1.0, 0.0).astype(BF)
        pick[s] = choice
        split = (devices, tile, degrees)
        e = turned(((1,), (1,)), choice, em_ref[...]).reshape(split)
        p = turned(((1,), (1,)), choice, le_ref[...]).reshape(split)
        both = jnp.concatenate([e, p], axis=1).astype(BF)
        out1[s] = both.reshape(order_size, blk_size, 2 * tile, degrees)
        land1[s, order_pos, blk] = out1[s, order_pos, blk]

    for s in range(group):
        arrange(s)
        if s == 0:
            pl.semaphore_wait(barrier, devices - 1)
        send_all(first, s)

    amplitude = math.sqrt(2.0 / lmax)
    chunk = 64

    def make_table(i, carry):
        begin = pl.multiple_of(i * chunk, chunk)
        q = i * chunk + lax.broadcasted_iota(jnp.int32, (chunk, 1), 0)
        colat = 2 * (2 * lax.rem(q, quarter) + lax.div(q, quarter)) + 1
        step = 4 * lax.broadcasted_iota(jnp.int32, (1, half), 1)
        sb, cb = sin_cos(colat * step, full)
        k = lax.broadcasted_iota(jnp.int32, (1, 128), 1)
        start = 2 * degrees * lax.rem(k, low) + 2 * lax.div(k, low) + 1
        sa, ca = sin_cos(colat * start, full)
        sa, ca = sa * amplitude, ca * amplitude
        for n in range(2 * low):
            at = slice(n * half, (n + 1) * half)
            s0, c0 = sa[:, n : n + 1], ca[:, n : n + 1]
            tab[pl.ds(begin, chunk), at] = (c0 * cb - s0 * sb).astype(BF)
            tab[pl.ds(couples + begin, chunk), at] = (s0 * cb + c0 * sb).astype(BF)
        return carry

    lax.fori_loop(0, couples // chunk, make_table, 0)

    row = lax.broadcasted_iota(jnp.int32, (rows, 1), 0)
    slot = lax.div(row, tile) * orders + lax.rem(row, orders)
    imaginary = lax.rem(lax.div(row, orders), 2) == 1
    order_total = m_ref.shape[1]
    slots = lax.broadcasted_iota(jnp.int32, (rows, order_total), 1)
    m = jnp.sum(
        jnp.where(slots == slot, m_ref[...].astype(F32), 0.0), axis=1, keepdims=True
    ).astype(jnp.int32)
    cm, sm = quarter_turns(m)
    factor = m.astype(F32) * (1.0 / lmax)

    lane = lax.broadcasted_iota(jnp.int32, (1, circle_total), 1)
    at_couple = lax.rem(lane, couples)
    near = 2 * lax.rem(at_couple, quarter) + lax.div(at_couple, quarter)
    circle = jnp.where(lane < couples, near, circle_total - 1 - near)
    ps, pc = sin_cos(2 * (2 * circle + 1), full)

    index_t = ci_ref[...].astype(F32).T
    weight_t = cw_ref[...].T
    circle_f = circle.astype(F32)
    total = jnp.zeros((8, circle_total), F32)
    for k in range(ci_ref.shape[0]):
        for g in range(ci_ref.shape[1] // 8):
            at = slice(8 * g, 8 * g + 8)
            total += jnp.where(index_t[at, k : k + 1] == circle_f, weight_t[at, k : k + 1], 0.0)
    wlane[...] = jnp.sum(total, axis=0, keepdims=True)

    scaling = 1.0 / math.sqrt(order_total)
    turn = 2 * lmax
    longitude = lax.broadcasted_iota(jnp.int32, (1, LONGS), 1)
    for parity in range(2):
        si, co = sin_cos(m * (2 * longitude + parity), 2 * turn)
        si, co = si * scaling, co * scaling
        straight = jnp.where(imaginary, -si, co)
        crossed = jnp.where(imaginary, -co, -si)
        waves_t[parity] = straight.astype(BF)
        waves[parity, 0] = straight.T.astype(BF)
        waves[parity, 1] = crossed.T.astype(BF)

    kappa = 2.0 / (2.0 * lmax)
    within_deg = lax.broadcasted_iota(jnp.int32, (1, degrees), 1)
    within_deg = 2 * lax.rem(within_deg, half) + lax.div(within_deg, half)

    def process(s, carry):
        await_all(first, s)

        def fold(b, inner):
            deg = b * degrees + within_deg
            far = deg + low * degrees
            wd = (2 * deg + 1).astype(F32) * (1.0 / (2.0 * lmax))
            wf = (2 * far + 1).astype(F32) * (1.0 / (2.0 * lmax))
            one, two = land1[s, :, b].astype(F32), land1[s, :, b + low].astype(F32)
            for k in range(2):
                x = one[:, k * tile : (k + 1) * tile].reshape(rows, degrees)
                z = two[:, k * tile : (k + 1) * tile].reshape(rows, degrees)
                x = jnp.where(deg >= m, x, 0.0)
                z = jnp.where(far >= m, z, 0.0)
                flat, steep = (x - z).astype(BF), (wd * x - wf * z).astype(BF)
                for parity in range(2):
                    to = pl.ds(pl.multiple_of(parity * span + b * half, half), half)
                    of = slice(parity * half, (parity + 1) * half)
                    xs[2 * k * rows : (2 * k + 1) * rows, to] = flat[:, of]
                    xs[(2 * k + 1) * rows : (2 * k + 2) * rows, to] = steep[:, of]
            return inner

        lax.fori_loop(0, low, fold, 0)
        even = turned(((1,), (1,)), xs[:, :span], tab[:, :span])
        odd = turned(((1,), (1,)), xs[:, span:], tab[:, span:])
        plus, minus = even + odd, even - odd
        c_all = jnp.concatenate([plus[:, :couples], minus[:, couples:]], axis=1)
        s_all = jnp.concatenate([plus[:, couples:], minus[:, :couples]], axis=1)

        def turns(k):
            at = slice(k * rows, (k + 1) * rows)
            c0, s0 = c_all[at], s_all[at]
            return cm * c0 + sm * s0, cm * s0 - sm * c0

        a, b = turns(0)
        gc, gs = turns(1)
        la, _ = turns(2)
        _, lgs = turns(3)
        maps[0] = (-(pc * (gs + kappa * b) + ps * (gc + kappa * a))).astype(BF)
        maps[1] = (-(pc * (gs - kappa * b) - ps * (gc - kappa * a))).astype(BF)
        maps[2] = (-lgs).astype(BF)
        maps[3] = (factor * (pc * a - ps * b)).astype(BF)
        maps[4] = (factor * (pc * a + ps * b)).astype(BF)
        maps[5] = (factor * la).astype(BF)

        def pixels(n, inner):
            at = pl.ds(pl.multiple_of(n * quarter, quarter), quarter)
            parity = lax.rem(n + lax.div(n, 2), 2)
            qt, ut, dt = (
                jnp.dot(waves[parity, 0], maps[k, :, at], preferred_element_type=F32) for k in range(3)
            )
            qp, up, dp = (
                jnp.dot(waves[parity, 1], maps[k, :, at], preferred_element_type=F32) for k in range(3, 6)
            )
            dq = (dt * qt + dp * qp).astype(BF)
            du = (dt * ut + dp * up).astype(BF)
            w = wlane[:, at]
            ana[0, :, at] = (jnp.dot(waves_t[parity], dq, preferred_element_type=F32) * w).astype(BF)
            ana[1, :, at] = (jnp.dot(waves_t[parity], du, preferred_element_type=F32) * w).astype(BF)
            return inner

        lax.fori_loop(0, 4, pixels, 0)
        gq, gu = ana[0].astype(F32), ana[1].astype(F32)
        x1, y1 = pc * (gq + gu), ps * (gq - gu)
        x2, y2 = pc * (gu - gq), ps * (gu + gq)
        for k, (x, y) in enumerate(((x1, y1), (x2, y2))):
            at = slice(k * rows, (k + 1) * rows)
            up, vp = cm * x + sm * y, sm * x - cm * y
            near_u, far_u = up[:, :couples], up[:, couples:]
            near_v, far_v = vp[:, :couples], vp[:, couples:]
            pairs[0, at, :couples] = (near_u + far_v).astype(BF)
            pairs[0, at, couples:] = (near_v + far_u).astype(BF)
            pairs[1, at, :couples] = (near_u - far_v).astype(BF)
            pairs[1, at, couples:] = (near_v - far_u).astype(BF)

        def give(b, inner):
            sums = [
                jnp.dot(
                    pairs[parity],
                    tab[:, pl.ds(pl.multiple_of(parity * span + b * half, half), half)],
                    preferred_element_type=F32,
                )
                for parity in range(2)
            ]
            sums = jnp.concatenate(sums, axis=1)
            deg = b * degrees + within_deg
            split = (order_size, tile, degrees)
            grad, curl = sums[:rows], sums[rows:]

            def packed(inside, sign):
                g = jnp.where(inside, sign * grad, 0.0).reshape(split)
                c = jnp.where(inside, sign * curl, 0.0).reshape(split)
                return jnp.concatenate([g, c], axis=1).astype(BF)

            out2[s, :, b] = packed(deg >= m, 1.0)
            out2[s, :, b + low] = packed(deg + low * degrees >= m, -1.0)
            return inner

        lax.fori_loop(0, low, give, 0)
        land2[s, order_pos, blk] = out2[s, order_pos, blk]
        send_all(second, s)
        return carry

    lax.fori_loop(0, group, process, 0)

    for s in range(group):
        await_all(second, s)
        got = land2[s].astype(F32).reshape(devices, 2 * tile, degrees)
        for k, ref in enumerate((grad_ref, curl_ref)):
            z = got[:, k * tile : (k + 1) * tile].reshape(devices * tile, degrees).astype(BF)
            value = turned(((0,), (0,)), z, pick[s])
            if s:
                value = value + ref[...].astype(F32)
            ref[...] = value.astype(BF)

    for s in range(group):
        sent_all(first, s)
        sent_all(second, s)


def by_realization(order_size, blk_size, emode_coeffs, lensing_coeffs, order_values, circle_indices, circle_weights):
    degrees, orders, csims = emode_coeffs.shape
    lmax = degrees * blk_size
    circle_total = circle_indices.shape[0]
    devices = order_size * blk_size
    group = csims // 2 // devices
    width = orders * csims
    tile = 2 * orders
    rows = order_size * tile

    def parted(coeffs):
        return coeffs.reshape(degrees // 2, 2, width).transpose(1, 0, 2).reshape(degrees, width)

    def joined(values):
        return values.reshape(2, degrees // 2, orders, csims).transpose(1, 0, 2, 3).reshape(degrees, orders, csims)

    dma = pltpu.SemaphoreType.DMA
    mail = pltpu.VMEM((group, order_size, blk_size, 2 * tile, degrees), BF)
    box = dma((group, order_size, blk_size))
    grad, curl = pl.pallas_call(
        functools.partial(
            realization_kernel, lmax, circle_total, order_size, blk_size, orders, csims, group
        ),
        out_shape=[jax.ShapeDtypeStruct((degrees, width), BF)] * 2,
        in_specs=[VMEM] * 5,
        out_specs=[VMEM, VMEM],
        scratch_shapes=[
            pltpu.VMEM((group, devices * tile, width), BF),
            mail, mail, mail, mail,
            pltpu.VMEM((circle_total, lmax // 2), BF),
            pltpu.VMEM((4 * rows, lmax // 2), BF),
            pltpu.VMEM((6, rows, circle_total), BF),
            pltpu.VMEM((2, 2, LONGS, rows), BF),
            pltpu.VMEM((2, rows, LONGS), BF),
            pltpu.VMEM((2, rows, circle_total), BF),
            pltpu.VMEM((2, 2 * rows, circle_total), BF),
            pltpu.VMEM((1, circle_total), F32),
            box, box, box, box,
        ],
        compiler_params=pltpu.CompilerParams(
            vmem_limit_bytes=48 << 20, collective_id=2, has_side_effects=True
        ),
        name="remap",
    )(
        parted(emode_coeffs),
        parted(lensing_coeffs),
        order_values.reshape(1, -1),
        circle_indices.reshape(-1, 128),
        circle_weights.reshape(-1, 128),
    )
    return joined(grad), joined(curl)


def splits_by_realization(order_size, blk_size, emode_coeffs, circle_indices):
    degrees, orders, csims = emode_coeffs.shape
    circle_total = circle_indices.shape[0]
    return (
        (csims // 2) % (order_size * blk_size) == 0
        and orders == 4
        and blk_size % 2 == 0
        and degrees % 256 == 0
        and degrees * blk_size == 4 * circle_total
        and circle_total % 512 == 0
    )


def body(order_size, blk_size, *arrays):
    if splits_by_realization(order_size, blk_size, arrays[0], arrays[3]):
        return by_realization(order_size, blk_size, *arrays)
    return by_circle(order_size, blk_size, *arrays)


def solution(mesh):
    in_specs = (P("blk", "order", None), P("blk", "order", None), P(), P(), P())
    out_specs = (P("blk", "order", None), P("blk", "order", None))
    sizes = (mesh.shape["order"], mesh.shape["blk"])
    return jax.shard_map(
        functools.partial(body, *sizes), mesh=mesh, in_specs=in_specs, out_specs=out_specs, check_vma=False
    )
```

```python
import functools
import math

import jax
import jax.numpy as jnp
from jax import lax
from jax.experimental import pallas as pl
from jax.experimental.pallas import tpu as pltpu
from jax.sharding import PartitionSpec as P

LONGS = 256
BF = jnp.bfloat16
F32 = jnp.float32
MESH = pl.DeviceIdType.MESH


def wrap(value, period):
    if period & (period - 1) == 0:
        return value & (period - 1)
    return jnp.mod(value, period)


def sin_cos(steps, period):
    quarter = period // 4
    steps = wrap(steps, period)
    turn = (steps + quarter // 2) // quarter if quarter & (quarter - 1) else (steps + quarter // 2) >> (quarter.bit_length() - 1)
    x = (steps - turn * quarter).astype(F32) * (2.0 * math.pi / period)
    x2 = x * x
    s = x * (1.0 + x2 * (-1.0 / 6 + x2 * (1.0 / 120 + x2 * (-1.0 / 5040 + x2 * (1.0 / 362880)))))
    c = 1.0 + x2 * (-0.5 + x2 * (1.0 / 24 + x2 * (-1.0 / 720 + x2 * (1.0 / 40320))))
    odd = (turn & 1) == 1
    sine = jnp.where(odd, c, s)
    cosine = jnp.where(odd, s, c)
    sine = jnp.where((turn & 2) == 2, -sine, sine)
    cosine = jnp.where(((turn + 1) & 2) == 2, -cosine, cosine)
    return sine, cosine


def quarter_turns(order):
    turn = order & 3
    c = jnp.where(turn == 0, 1.0, jnp.where(turn == 2, -1.0, 0.0)).astype(F32)
    s = jnp.where(turn == 1, 1.0, jnp.where(turn == 3, -1.0, 0.0)).astype(F32)
    return c, s


def neighbours(order_size, line):
    order_pos, blk = lax.axis_index("order"), lax.axis_index("blk")
    h, y = lax.div(blk, 2), lax.rem(blk, 2)
    pair = blk + 1 - 2 * y
    peers = [lax.rem(order_pos + k, order_size) for k in range(1, order_size)]
    return order_pos, blk, h, y, pair, peers


def greet(order_size, line):
    order_pos, blk, h, y, pair, peers = neighbours(order_size, line)
    barrier = pltpu.get_barrier_semaphore()

    @pl.when(h > 0)
    def _():
        pl.semaphore_signal(barrier, inc=1, device_id={"blk": blk - 2}, device_id_type=MESH)

    @pl.when(h < line - 1)
    def _():
        pl.semaphore_signal(barrier, inc=1, device_id={"blk": blk + 2}, device_id_type=MESH)

    pl.semaphore_signal(barrier, inc=1, device_id={"blk": pair}, device_id_type=MESH)
    for peer in peers:
        pl.semaphore_signal(barrier, inc=1, device_id={"order": peer}, device_id_type=MESH)
    ends = jnp.where(h > 0, 1, 0) + jnp.where(h < line - 1, 1, 0)
    pl.semaphore_wait(barrier, order_size + ends)


def remote(src, dst, send, recv, device):
    return pltpu.make_async_remote_copy(
        src_ref=src, dst_ref=dst, send_sem=send, recv_sem=recv, device_id=device, device_id_type=MESH
    )


def synth_kernel(
    lmax, circle_total, line, order_size, orders, csims,
    m_ref, r_ref, line_ref, e_ref, p_ref, out_ref,
    held, land, tab, acc, own, ysend, yrecv, asend, lens, ltab, lpart, csend, crecv,
    zs, zr, ys, yr, as_, ar, ls, lr, cs, cr,
):
    order_pos, blk, h, y, pair, peers = neighbours(order_size, line)
    rows = e_ref.shape[1]
    circles = r_ref.shape[0] // 2
    part = circles // order_size
    amplitude = math.sqrt(2.0 / lmax)
    colat = 2 * r_ref[...] + 1

    def along(src, block, o, way):
        return remote(
            src, held.at[block, o], zs.at[way, block, o], zr.at[block, o], {"blk": blk - 2 + 4 * way}
        )

    def send_own(o):
        @pl.when(h > 0)
        def _():
            along(e_ref.at[o], h, o, 0).start()

        @pl.when(h < line - 1)
        def _():
            along(e_ref.at[o], h, o, 1).start()

    def across(o):
        return remote(ysend.at[o], yrecv.at[o], ys.at[o], yr.at[o], {"blk": pair})

    def spread(o, peer, source):
        begin = pl.multiple_of(peer * part, part)
        return remote(
            asend.at[o, pl.ds(begin, part)], land.at[source * orders + o],
            as_.at[peer, o], ar.at[source, o], {"order": peer},
        )

    def share(o, lane):
        begin = pl.multiple_of(lane * rows, rows)
        return remote(
            p_ref.at[o], lens.at[o, pl.ds(begin, rows)], ls.at[o], lr.at[o], {"blk": pair}
        )

    def chain(way, target, o):
        return remote(
            csend.at[way, target, o], crecv.at[way, target, o],
            cs.at[way, target, o], cr.at[way, target, o], {"blk": blk - 2 + 4 * way},
        )

    greet(order_size, line)
    for o in range(orders):
        share(o, y).start()
        send_own(o)
    lens[:, pl.ds(pl.multiple_of(y * rows, rows), rows), :] = p_ref[...]

    def make_table(block, carry):
        degree = (2 * block + y) * rows + lax.broadcasted_iota(jnp.int32, (1, rows), 1)
        freq = 2 * degree + 1
        sine, cosine = sin_cos(colat * freq, 8 * circle_total)
        sine, cosine = sine * amplitude, cosine * amplitude
        weight = freq.astype(F32) / (2.0 * lmax)
        for k, value in enumerate((cosine, sine, cosine * weight, sine * weight)):
            tab[block, 2 * k * circles : 2 * (k + 1) * circles, :] = value.astype(BF)
        return carry

    def make_lens_table(target, carry):
        degree = 2 * h * rows + lax.broadcasted_iota(jnp.int32, (1, 2 * rows), 1)
        freq = 2 * degree + 1
        sine, cosine = sin_cos((2 * line_ref[target] + 1) * freq, 8 * circle_total)
        sine, cosine = sine * amplitude, cosine * amplitude
        weight = freq.astype(F32) / (2.0 * lmax)
        for k, value in enumerate((cosine, sine, sine * weight, cosine * weight)):
            ltab[k, target] = value.astype(BF)
        return carry

    lax.fori_loop(0, line, make_lens_table, 0)
    lax.fori_loop(0, line, make_table, 0)
    ps, pc = sin_cos(colat * 2, 8 * circle_total)
    kappa = 2.0 / (2.0 * lmax)

    def product(values, block, o):
        degree = (2 * block + y) * rows + lax.broadcasted_iota(jnp.int32, values.shape, 0)
        values = jnp.where(degree >= m_ref[o], values, jnp.zeros_like(values))
        return jnp.dot(tab[block], values, preferred_element_type=F32)

    def finish(o):
        across(o).wait_recv()
        cut = 4 * csims
        asend[o, :, :cut] = (own[o] + yrecv[o].astype(F32)).astype(BF)
        asend[o, :, cut:] = lpart[o, h].astype(BF)
        for peer in peers:
            spread(o, peer, order_pos).start()
        begin = pl.multiple_of(order_pos * part, part)
        land[order_pos * orders + o] = asend[o, pl.ds(begin, part)]

    def lens_sums(o):
        share(o, 1 - y).wait_recv()
        m = m_ref[o]
        cm, sm = quarter_turns(m)
        values = lens[o]
        degree = 2 * h * rows + lax.broadcasted_iota(jnp.int32, values.shape, 0)
        values = jnp.where(degree >= m, values, jnp.zeros_like(values))
        flat, split = (line * circles, 2 * rows), (line, circles, csims)
        theta = jnp.dot(ltab[2 + (m & 1)].reshape(flat), values, preferred_element_type=F32)
        lpart[o, :, :, :csims] = ((sm - cm) * theta).reshape(split)
        flow = jnp.dot(ltab[m & 1].reshape(flat), values, preferred_element_type=F32)
        lpart[o, :, :, csims:] = ((cm + sm) * (m.astype(F32) * (1.0 / lmax)) * flow).reshape(split)

    def stage(t, o):
        def leftward(target, carry):
            @pl.when((target <= h) & (h < line - 1))
            def _():
                chain(0, target, o).wait_recv()
                lpart[o, target] += crecv[0, target, o].astype(F32)

            @pl.when(target < h)
            def _():
                csend[0, target, o] = lpart[o, target].astype(BF)
                chain(0, target, o).start()

            return carry

        def rightward(target, carry):
            @pl.when((target >= h) & (h > 0))
            def _():
                chain(1, target, o).wait_recv()
                lpart[o, target] += crecv[1, target, o].astype(F32)

            @pl.when(target > h)
            def _():
                csend[1, target, o] = lpart[o, target].astype(BF)
                chain(1, target, o).start()

            return carry

        @pl.when(h == line - 1 - t)
        def _():
            lax.fori_loop(0, line, leftward, 0)

        @pl.when(h == t)
        def _():
            lax.fori_loop(0, line, rightward, 0)

    def hop(s, o):
        after, before = h + s, h - s

        @pl.when(after < line)
        def _():
            along(held.at[after, o], after, o, 0).wait_recv()

            @pl.when(h > 0)
            def _():
                along(held.at[after, o], after, o, 0).start()

        @pl.when(before >= 0)
        def _():
            along(held.at[before, o], before, o, 1).wait_recv()

            @pl.when(h < line - 1)
            def _():
                along(held.at[before, o], before, o, 1).start()

        @pl.when(after < line)
        def _():
            acc[o] += product(held[after, o], after, o)

        @pl.when(before >= 0)
        def _():
            acc[o] += product(held[before, o], before, o)

    def emode_maps(o):
        cm, sm = quarter_turns(m_ref[o])
        factor = m_ref[o].astype(F32) * (1.0 / lmax)
        c0, s0, gc0, gs0 = (acc[o, 2 * k * circles : 2 * (k + 1) * circles] for k in range(4))
        a, b = cm * c0 + sm * s0, cm * s0 - sm * c0
        gc, gs = cm * gc0 + sm * gs0, cm * gs0 - sm * gc0
        maps = (
            -(pc * (gs + kappa * b) + ps * (gc + kappa * a)),
            -(pc * (gs - kappa * b) - ps * (gc - kappa * a)),
            factor * (pc * a - ps * b),
            factor * (pc * a + ps * b),
        )
        for k, value in enumerate(maps):
            at = slice(k * csims, (k + 1) * csims)
            own[o, :, at] = value[:circles]
            ysend[o, :, at] = value[circles:].astype(BF)
        across(o).start()

    def one_phase(s, outer):
        def one_order(o, carry):
            @pl.when(s < line)
            def _():
                hop(s, o)

            @pl.when(s == 1)
            def _():
                lens_sums(o)

            @pl.when(s == line - 1)
            def _():
                emode_maps(o)

            stage(s - 1, o)

            @pl.when(s == line)
            def _():
                finish(o)

            return carry

        return lax.fori_loop(0, orders, one_order, outer)

    def own_product(o, carry):
        acc[o] = product(e_ref[o], h, o)
        return carry

    lax.fori_loop(0, orders, own_product, 0)
    lax.fori_loop(1, line + 1, one_phase, 0)

    def settle(o, carry):
        across(o).wait_send()
        share(o, y).wait_send()
        for peer in peers:
            spread(o, peer, order_pos).wait_send()
            spread(o, peer, peer).wait_recv()

        def sent(block, inner):
            @pl.when((h > 0) & (block >= h))
            def _():
                along(held.at[block, o], block, o, 0).wait_send()

            @pl.when((h < line - 1) & (block <= h))
            def _():
                along(held.at[block, o], block, o, 1).wait_send()

            @pl.when(block < h)
            def _():
                chain(0, block, o).wait_send()

            @pl.when(block > h)
            def _():
                chain(1, block, o).wait_send()

            return inner

        lax.fori_loop(0, line, sent, 0)
        return carry

    lax.fori_loop(0, orders, settle, 0)
    out_ref[...] = land[...]


def pixel_kernel(orders, csims, par_ref, w_ref, m_ref, f_ref, ft_ref, out_ref):
    count = m_ref.shape[0]
    sims = csims // 2
    low = lax.broadcasted_iota(jnp.int32, (orders, csims), 1) < sims
    begin = pl.program_id(0) * count

    def halves(x, y):
        first = jnp.where(low, x, pltpu.roll(y, sims, 1))
        second = jnp.where(low, pltpu.roll(x, sims, 1), y)
        return first, second

    for c in range(count):
        qt, ut, qc, uc, dt, dc = (
            m_ref[c, :, k * csims : (k + 1) * csims].astype(F32) for k in range(6)
        )
        t_re, t_im = halves(qt, ut)
        c_re, c_im = halves(qc, uc)
        dt_re, dt_im = halves(dt, dt)
        dc_re, dc_im = halves(dc, dc)
        real = jnp.concatenate([t_re, -c_im, dt_re, -dc_im], axis=1)
        imag = jnp.concatenate([t_im, c_re, dt_im, dc_re], axis=1)
        arranged = jnp.concatenate([real, imag], axis=0).astype(BF)
        parity = par_ref[begin + c]
        pixels = jnp.dot(ft_ref[parity], arranged, preferred_element_type=F32)
        deflected = (
            pixels[:, 2 * csims : 3 * csims] * pixels[:, :csims]
            + pixels[:, 3 * csims :] * pixels[:, csims : 2 * csims]
        ).astype(BF)
        analysed = jnp.dot(f_ref[parity], deflected, preferred_element_type=F32) * w_ref[begin + c]
        gq, gu = halves(analysed[:orders], analysed[orders:])
        out_ref[c, :, :csims] = gq.astype(BF)
        out_ref[c, :, csims:] = gu.astype(BF)


def adjoint_kernel(
    lmax, circle_total, line, order_size, orders, csims,
    m_ref, r_ref, rc_ref, w_ref, grad_ref, curl_ref,
    gath, tab, acc, zs, zr, ys, yr, as_, ar,
):
    order_pos, blk, h, y, pair, peers = neighbours(order_size, line)
    degrees = grad_ref.shape[0]
    circles = gath.shape[2]
    part = w_ref.shape[1]
    amplitude = math.sqrt(2.0 / lmax)

    def back(peer, source):
        begin = pl.multiple_of(source * part, part)
        return remote(
            w_ref.at[pl.ds(peer * orders, orders)], gath.at[blk, :, pl.ds(begin, part)],
            as_.at[peer], ar.at[source], {"order": peer},
        )

    def along(line_at, way):
        block = gath.at[2 * line_at + y]
        return remote(block, block, zs.at[way, line_at], zr.at[line_at], {"blk": blk - 2 + 4 * way})

    def across(line_at, lane):
        block = gath.at[2 * line_at + lane]
        return remote(block, block, ys.at[line_at], yr.at[line_at], {"blk": pair})

    greet(order_size, line)
    for peer in peers:
        back(peer, order_pos).start()
    begin = pl.multiple_of(order_pos * part, part)
    gath[blk, :, pl.ds(begin, part), :] = w_ref[pl.ds(order_pos * orders, orders)]

    def make_table(block, carry):
        degree = blk * degrees + lax.broadcasted_iota(jnp.int32, (degrees, 1), 0)
        sine, cosine = sin_cos((2 * degree + 1) * (2 * r_ref[block] + 1), 8 * circle_total)
        tab[block, :, :circles] = (cosine * amplitude).astype(BF)
        tab[block, :, circles:] = (sine * amplitude).astype(BF)
        return carry

    lax.fori_loop(0, line // 2, make_table, 0)

    def add(block):
        ps, pc = sin_cos(2 * (2 * rc_ref[block] + 1), 8 * circle_total)
        ups, vps = [], []
        for o in range(orders):
            cm, sm = quarter_turns(m_ref[o])
            gq = gath[block, o, :, :csims].astype(F32)
            gu = gath[block, o, :, csims:].astype(F32)
            x1, y1 = pc * (gq + gu), ps * (gq - gu)
            x2, y2 = pc * (gu - gq), ps * (gu + gq)
            ups += [(cm * x1 + sm * y1).astype(BF), (cm * x2 + sm * y2).astype(BF)]
            vps += [(sm * x1 - cm * y1).astype(BF), (sm * x2 - cm * y2).astype(BF)]
        values = jnp.concatenate(
            [jnp.concatenate(ups, axis=1), jnp.concatenate(vps, axis=1)], axis=0
        )
        acc[...] += jnp.dot(tab[block], values, preferred_element_type=F32)

    for peer in peers:
        back(peer, peer).wait_recv()

    @pl.when(h > 0)
    def _():
        along(h, 0).start()

    @pl.when(h < line - 1)
    def _():
        along(h, 1).start()

    across(h, y).start()
    lax.fori_loop(line // 2, 2 * line, make_table, 0)
    acc[...] = jnp.zeros_like(acc)

    def hop(s, carry):
        after, before = h + s, h - s

        @pl.when((s > 0) & (after < line))
        def _():
            along(after, 0).wait_recv()

            @pl.when(h > 0)
            def _():
                along(after, 0).start()

            across(after, y).start()

        @pl.when((s > 0) & (before >= 0))
        def _():
            along(before, 1).wait_recv()

            @pl.when(h < line - 1)
            def _():
                along(before, 1).start()

            across(before, y).start()

        @pl.when(after < line)
        def _():
            add(2 * after + y)

        @pl.when((s > 0) & (before >= 0))
        def _():
            add(2 * before + y)

        return carry

    lax.fori_loop(0, line, hop, 0)

    def cross(s, carry):
        after, before = h + s, h - s

        @pl.when(after < line)
        def _():
            across(after, 1 - y).wait_recv()
            add(2 * after + 1 - y)

        @pl.when((s > 0) & (before >= 0))
        def _():
            across(before, 1 - y).wait_recv()
            add(2 * before + 1 - y)

        return carry

    lax.fori_loop(0, line, cross, 0)
    for peer in peers:
        back(peer, order_pos).wait_send()

    def settle(line_at, carry):
        across(line_at, y).wait_send()

        @pl.when((h > 0) & (line_at >= h))
        def _():
            along(line_at, 0).wait_send()

        @pl.when((h < line - 1) & (line_at <= h))
        def _():
            along(line_at, 1).wait_send()

        return carry

    lax.fori_loop(0, line, settle, 0)
    rows = blk * degrees + lax.broadcasted_iota(jnp.int32, (degrees, csims), 0)
    for o in range(orders):
        inside = rows >= m_ref[o]
        at = slice(o * csims, (o + 1) * csims)
        grad = acc[:, 2 * o * csims : (2 * o + 1) * csims]
        curl = acc[:, (2 * o + 1) * csims : (2 * o + 2) * csims]
        grad_ref[:, at] = jnp.where(inside, grad, 0.0).astype(BF)
        curl_ref[:, at] = jnp.where(inside, curl, 0.0).astype(BF)


def longitude_table(lmax, parity, order_list):
    full_circle = 2 * lmax
    longitude = jnp.arange(LONGS, dtype=jnp.int32)
    phase_steps = order_list[None, :, None] * (2 * longitude[None, None, :] + parity[:, None, None])
    phase_steps = jnp.mod(phase_steps, 2 * full_circle)
    angles = phase_steps.astype(jnp.float32) * (math.pi / full_circle)
    scaling = 1.0 / math.sqrt(order_list.shape[0])
    fourier = jnp.concatenate([jnp.cos(angles) * scaling, -jnp.sin(angles) * scaling], axis=1)
    return fourier.astype(BF)


def divisor(total, limit):
    return next(k for k in range(min(total, limit), 0, -1) if total % k == 0)


SMEM = pl.BlockSpec(memory_space=pltpu.SMEM)
VMEM = pl.BlockSpec(memory_space=pltpu.VMEM)
PARAMS = pltpu.CompilerParams(vmem_limit_bytes=48 << 20)


def by_circle(order_size, blk_size, emode_coeffs, lensing_coeffs, order_values, circle_indices, circle_weights):
    degree_local, orders, csims = emode_coeffs.shape
    lmax = degree_local * blk_size
    circle_total = circle_indices.shape[0]
    order_total = order_values.shape[0]
    circles = circle_total // blk_size
    order_pos = lax.axis_index("order")
    block_pos = lax.axis_index("blk")
    my_orders = lax.dynamic_slice_in_dim(order_values, order_pos * orders, orders)
    width = orders * csims
    line = blk_size // 2
    blocks = circle_indices.reshape(blk_size, circles)
    pair_circles = jnp.concatenate(
        [
            lax.dynamic_index_in_dim(blocks, block_pos, 0, keepdims=False),
            lax.dynamic_index_in_dim(blocks, block_pos ^ 1, 0, keepdims=False),
        ]
    )
    line_circles = lax.dynamic_index_in_dim(
        circle_indices.reshape(line, 2, circles), block_pos % 2, 1, keepdims=False
    )
    fourier = longitude_table(lmax, jnp.arange(2, dtype=jnp.int32), order_values)
    fourier_t = fourier.transpose(0, 2, 1)
    part = circles // order_size
    dma = pltpu.SemaphoreType.DMA
    spread = pl.pallas_call(
        functools.partial(synth_kernel, lmax, circle_total, line, order_size, orders, csims),
        out_shape=jax.ShapeDtypeStruct((order_total, part, 6 * csims), BF),
        in_specs=[SMEM, VMEM, VMEM, VMEM, VMEM],
        out_specs=VMEM,
        scratch_shapes=[
            pltpu.VMEM((line, orders, degree_local, csims), BF),
            pltpu.VMEM((order_total, part, 6 * csims), BF),
            pltpu.VMEM((line, 8 * circles, degree_local), BF),
            pltpu.VMEM((orders, 8 * circles, csims), F32),
            pltpu.VMEM((orders, circles, 4 * csims), F32),
            pltpu.VMEM((orders, circles, 4 * csims), BF),
            pltpu.VMEM((orders, circles, 4 * csims), BF),
            pltpu.VMEM((orders, circles, 6 * csims), BF),
            pltpu.VMEM((orders, 2 * degree_local, csims), BF),
            pltpu.VMEM((4, line, circles, 2 * degree_local), BF),
            pltpu.VMEM((orders, line, circles, 2 * csims), F32),
            pltpu.VMEM((2, line, orders, circles, 2 * csims), BF),
            pltpu.VMEM((2, line, orders, circles, 2 * csims), BF),
            dma((2, line, orders)),
            dma((line, orders)),
            dma((orders,)),
            dma((orders,)),
            dma((order_size, orders)),
            dma((order_size, orders)),
            dma((orders,)),
            dma((orders,)),
            dma((2, line, orders)),
            dma((2, line, orders)),
        ],
        compiler_params=pltpu.CompilerParams(
            vmem_limit_bytes=48 << 20, collective_id=0, has_side_effects=True
        ),
        name="synth",
    )(
        my_orders,
        pair_circles[:, None],
        line_circles[:, :, None],
        emode_coeffs.transpose(1, 0, 2),
        lensing_coeffs.transpose(1, 0, 2),
    )
    spread = spread.transpose(1, 0, 2)
    begin = block_pos * circles + order_pos * part
    part_circles = lax.dynamic_slice_in_dim(circle_indices, begin, part)
    part_weights = lax.dynamic_slice_in_dim(circle_weights, begin, part)
    count = divisor(part, 8)
    weighted = pl.pallas_call(
        functools.partial(pixel_kernel, order_total, csims),
        out_shape=jax.ShapeDtypeStruct((part, order_total, 2 * csims), BF),
        grid=(part // count,),
        in_specs=[
            SMEM,
            SMEM,
            pl.BlockSpec((count, order_total, 6 * csims), lambda i: (i, 0, 0)),
            pl.BlockSpec((2, 2 * order_total, LONGS), lambda i: (0, 0, 0)),
            pl.BlockSpec((2, LONGS, 2 * order_total), lambda i: (0, 0, 0)),
        ],
        out_specs=pl.BlockSpec((count, order_total, 2 * csims), lambda i: (i, 0, 0)),
        compiler_params=PARAMS,
        name="pixels",
    )(jnp.mod(part_circles, 2), part_weights, spread, fourier, fourier_t)
    grad, curl = pl.pallas_call(
        functools.partial(adjoint_kernel, lmax, circle_total, line, order_size, orders, csims),
        out_shape=[jax.ShapeDtypeStruct((degree_local, width), BF)] * 2,
        in_specs=[SMEM, VMEM, VMEM, VMEM],
        out_specs=[VMEM, VMEM],
        scratch_shapes=[
            pltpu.VMEM((blk_size, orders, circles, 2 * csims), BF),
            pltpu.VMEM((blk_size, degree_local, 2 * circles), BF),
            pltpu.VMEM((degree_local, 2 * width), F32),
            dma((2, line)),
            dma((line,)),
            dma((line,)),
            dma((line,)),
            dma((order_size,)),
            dma((order_size,)),
        ],
        compiler_params=pltpu.CompilerParams(
            vmem_limit_bytes=48 << 20, collective_id=1, has_side_effects=True
        ),
        name="adjoint",
    )(my_orders, blocks[:, None, :], blocks[:, :, None], weighted.transpose(1, 0, 2))
    return grad.reshape(emode_coeffs.shape), curl.reshape(emode_coeffs.shape)


def turned(dims, left, right):
    return lax.dot_general(left, right, (dims, ((), ())), preferred_element_type=F32)


def realization_kernel(
    lmax, circle_total, order_size, blk_size, orders, csims, group,
    em_ref, le_ref, m_ref, ci_ref, cw_ref, grad_ref, curl_ref,
    pick, out1, land1, out2, land2, tab, xs, maps, waves, waves_t, ana, pairs, wlane,
    s1, r1, s2, r2,
):
    order_pos, blk = lax.axis_index("order"), lax.axis_index("blk")
    devices = order_size * blk_size
    me = order_pos * blk_size + blk
    degrees = em_ref.shape[0]
    half = degrees // 2
    sims = csims // 2
    low = blk_size // 2
    span = low * half
    couples = circle_total // 2
    quarter = couples // 2
    rows = order_size * 2 * orders
    tile = 2 * orders
    full = 8 * circle_total
    width = orders * csims

    late_from = blk_size - blk_size // 4
    early = blk < late_from
    early_total = order_size * late_from
    late_total = devices - early_total

    def each(begin, end, act):
        def one(k, carry):
            b = begin + lax.div(k, order_size)
            o = lax.rem(order_pos + lax.rem(k, order_size), order_size)

            @pl.when((o != order_pos) | (b != blk))
            def _():
                act(o, b)

            return carry

        lax.fori_loop(0, (end - begin) * order_size, one, 0)

    def hand(src, dst, send, recv, s, o, b):
        return pltpu.make_async_remote_copy(
            src_ref=src.at[s, o, b], dst_ref=dst.at[s, order_pos, blk],
            send_sem=send.at[s, o, b], recv_sem=recv.at[s, order_pos, blk],
            device_id={"order": o, "blk": b}, device_id_type=MESH,
        )

    def arrival(src, dst, send, recv, s, o, b):
        return pltpu.make_async_remote_copy(
            src_ref=src.at[s, o, b], dst_ref=dst.at[s, o, b],
            send_sem=send.at[s, o, b], recv_sem=recv.at[s, o, b],
            device_id={"order": o, "blk": b}, device_id_type=MESH,
        )

    first = (out1, land1, s1, r1)
    second = (out2, land2, s2, r2)

    def send_to(args, s, begin, end):
        each(begin, end, lambda o, b: hand(*args, s, o, b).start())

    def send_all(args, s):
        each(0, blk_size, lambda o, b: hand(*args, s, o, b).start())

    def await_all(args, s):
        each(0, blk_size, lambda o, b: arrival(*args, s, o, b).wait_recv())

    def sent_all(args, s):
        each(0, blk_size, lambda o, b: hand(*args, s, o, b).wait_send())

    barrier = pltpu.get_barrier_semaphore()

    def hail(begin, end):
        each(
            begin, end,
            lambda o, b: pl.semaphore_signal(
                barrier, inc=1, device_id={"order": o, "blk": b}, device_id_type=MESH
            ),
        )

    @pl.when(early)
    def _():
        hail(0, late_from)

    @pl.when(jnp.logical_not(early))
    def _():
        hail(late_from, blk_size)

    def arrange(s):
        row = lax.broadcasted_iota(jnp.int32, (devices * tile, 1), 0)
        within = lax.rem(row, tile)
        column = (
            lax.rem(within, orders) * csims + lax.div(within, orders) * sims + lax.div(row, tile) * group + s
        )
        lane = lax.broadcasted_iota(jnp.int32, (devices * tile, width), 1)
        choice = jnp.where(lane == column, 1.0, 0.0).astype(BF)
        pick[s] = choice
        split = (devices, tile, degrees)
        e = turned(((1,), (1,)), choice, em_ref[...]).reshape(split)
        p = turned(((1,), (1,)), choice, le_ref[...]).reshape(split)
        both = jnp.concatenate([e, p], axis=1).astype(BF)
        out1[s] = both.reshape(order_size, blk_size, 2 * tile, degrees)
        land1[s, order_pos, blk] = out1[s, order_pos, blk]

    arrange(0)

    @pl.when(early)
    def _():
        pl.semaphore_wait(barrier, early_total - 1)
        hail(late_from, blk_size)
        send_to(first, 0, 0, late_from)

    @pl.when(jnp.logical_not(early))
    def _():
        pl.semaphore_wait(barrier, devices - 1)
        hail(0, late_from)
        send_to(first, 0, 0, blk_size)

    for s in range(1, group):
        arrange(s)

    @pl.when(early)
    def _():
        pl.semaphore_wait(barrier, late_total)
        send_to(first, 0, late_from, blk_size)

    for s in range(1, group):
        send_all(first, s)

    amplitude = math.sqrt(2.0 / lmax)
    chunk = 64

    def make_table(i, carry):
        begin = pl.multiple_of(i * chunk, chunk)
        q = i * chunk + lax.broadcasted_iota(jnp.int32, (chunk, 1), 0)
        colat = 2 * (2 * lax.rem(q, quarter) + lax.div(q, quarter)) + 1
        step = 4 * lax.broadcasted_iota(jnp.int32, (1, half), 1)
        sb, cb = sin_cos(colat * step, full)
        k = lax.broadcasted_iota(jnp.int32, (1, 128), 1)
        start = 2 * degrees * lax.rem(k, low) + 2 * lax.div(k, low) + 1
        sa, ca = sin_cos(colat * start, full)
        sa, ca = sa * amplitude, ca * amplitude
        for n in range(2 * low):
            at = slice(n * half, (n + 1) * half)
            s0, c0 = sa[:, n : n + 1], ca[:, n : n + 1]
            tab[pl.ds(begin, chunk), at] = (c0 * cb - s0 * sb).astype(BF)
            tab[pl.ds(couples + begin, chunk), at] = (s0 * cb + c0 * sb).astype(BF)
        return carry

    lax.fori_loop(0, couples // chunk, make_table, 0)

    row = lax.broadcasted_iota(jnp.int32, (rows, 1), 0)
    slot = lax.div(row, tile) * orders + lax.rem(row, orders)
    imaginary = lax.rem(lax.div(row, orders), 2) == 1
    order_total = m_ref.shape[1]
    slots = lax.broadcasted_iota(jnp.int32, (rows, order_total), 1)
    m = jnp.sum(
        jnp.where(slots == slot, m_ref[...].astype(F32), 0.0), axis=1, keepdims=True
    ).astype(jnp.int32)
    cm, sm = quarter_turns(m)
    factor = m.astype(F32) * (1.0 / lmax)

    lane = lax.broadcasted_iota(jnp.int32, (1, circle_total), 1)
    at_couple = lax.rem(lane, couples)
    near = 2 * lax.rem(at_couple, quarter) + lax.div(at_couple, quarter)
    circle = jnp.where(lane < couples, near, circle_total - 1 - near)
    ps, pc = sin_cos(2 * (2 * circle + 1), full)

    index_t = ci_ref[...].astype(F32).T
    weight_t = cw_ref[...].T
    circle_f = circle.astype(F32)
    total = jnp.zeros((8, circle_total), F32)
    for k in range(ci_ref.shape[0]):
        for g in range(ci_ref.shape[1] // 8):
            at = slice(8 * g, 8 * g + 8)
            total += jnp.where(index_t[at, k : k + 1] == circle_f, weight_t[at, k : k + 1], 0.0)
    wlane[...] = jnp.sum(total, axis=0, keepdims=True)

    scaling = 1.0 / math.sqrt(order_total)
    turn = 2 * lmax
    longitude = lax.broadcasted_iota(jnp.int32, (1, LONGS), 1)
    for parity in range(2):
        si, co = sin_cos(m * (2 * longitude + parity), 2 * turn)
        si, co = si * scaling, co * scaling
        straight = jnp.where(imaginary, -si, co)
        crossed = jnp.where(imaginary, -co, -si)
        waves_t[parity] = straight.astype(BF)
        waves[parity, 0] = straight.T.astype(BF)
        waves[parity, 1] = crossed.T.astype(BF)

    kappa = 2.0 / (2.0 * lmax)
    within_deg = lax.broadcasted_iota(jnp.int32, (1, degrees), 1)
    within_deg = 2 * lax.rem(within_deg, half) + lax.div(within_deg, half)

    def process(s, carry):
        await_all(first, s)

        def fold(b, inner):
            deg = b * degrees + within_deg
            far = deg + low * degrees
            wd = (2 * deg + 1).astype(F32) * (1.0 / (2.0 * lmax))
            wf = (2 * far + 1).astype(F32) * (1.0 / (2.0 * lmax))
            one, two = land1[s, :, b].astype(F32), land1[s, :, b + low].astype(F32)
            for k in range(2):
                x = one[:, k * tile : (k + 1) * tile].reshape(rows, degrees)
                z = two[:, k * tile : (k + 1) * tile].reshape(rows, degrees)
                x = jnp.where(deg >= m, x, 0.0)
                z = jnp.where(far >= m, z, 0.0)
                flat, steep = (x - z).astype(BF), (wd * x - wf * z).astype(BF)
                for parity in range(2):
                    to = pl.ds(pl.multiple_of(parity * span + b * half, half), half)
                    of = slice(parity * half, (parity + 1) * half)
                    xs[2 * k * rows : (2 * k + 1) * rows, to] = flat[:, of]
                    xs[(2 * k + 1) * rows : (2 * k + 2) * rows, to] = steep[:, of]
            return inner

        lax.fori_loop(0, low, fold, 0)
        even = turned(((1,), (1,)), xs[:, :span], tab[:, :span])
        odd = turned(((1,), (1,)), xs[:, span:], tab[:, span:])
        plus, minus = even + odd, even - odd
        c_all = jnp.concatenate([plus[:, :couples], minus[:, couples:]], axis=1)
        s_all = jnp.concatenate([plus[:, couples:], minus[:, :couples]], axis=1)

        def turns(k):
            at = slice(k * rows, (k + 1) * rows)
            c0, s0 = c_all[at], s_all[at]
            return cm * c0 + sm * s0, cm * s0 - sm * c0

        a, b = turns(0)
        gc, gs = turns(1)
        la, _ = turns(2)
        _, lgs = turns(3)
        maps[0] = (-(pc * (gs + kappa * b) + ps * (gc + kappa * a))).astype(BF)
        maps[1] = (-(pc * (gs - kappa * b) - ps * (gc - kappa * a))).astype(BF)
        maps[2] = (-lgs).astype(BF)
        maps[3] = (factor * (pc * a - ps * b)).astype(BF)
        maps[4] = (factor * (pc * a + ps * b)).astype(BF)
        maps[5] = (factor * la).astype(BF)

        def pixels(n, inner):
            at = pl.ds(pl.multiple_of(n * quarter, quarter), quarter)
            parity = lax.rem(n + lax.div(n, 2), 2)
            qt, ut, dt = (
                jnp.dot(waves[parity, 0], maps[k, :, at], preferred_element_type=F32) for k in range(3)
            )
            qp, up, dp = (
                jnp.dot(waves[parity, 1], maps[k, :, at], preferred_element_type=F32) for k in range(3, 6)
            )
            dq = (dt * qt + dp * qp).astype(BF)
            du = (dt * ut + dp * up).astype(BF)
            w = wlane[:, at]
            ana[0, :, at] = (jnp.dot(waves_t[parity], dq, preferred_element_type=F32) * w).astype(BF)
            ana[1, :, at] = (jnp.dot(waves_t[parity], du, preferred_element_type=F32) * w).astype(BF)
            return inner

        lax.fori_loop(0, 4, pixels, 0)
        gq, gu = ana[0].astype(F32), ana[1].astype(F32)
        x1, y1 = pc * (gq + gu), ps * (gq - gu)
        x2, y2 = pc * (gu - gq), ps * (gu + gq)
        for k, (x, y) in enumerate(((x1, y1), (x2, y2))):
            at = slice(k * rows, (k + 1) * rows)
            up, vp = cm * x + sm * y, sm * x - cm * y
            near_u, far_u = up[:, :couples], up[:, couples:]
            near_v, far_v = vp[:, :couples], vp[:, couples:]
            pairs[0, at, :couples] = (near_u + far_v).astype(BF)
            pairs[0, at, couples:] = (near_v + far_u).astype(BF)
            pairs[1, at, :couples] = (near_u - far_v).astype(BF)
            pairs[1, at, couples:] = (near_v - far_u).astype(BF)

        def give(b, inner):
            sums = [
                jnp.dot(
                    pairs[parity],
                    tab[:, pl.ds(pl.multiple_of(parity * span + b * half, half), half)],
                    preferred_element_type=F32,
                )
                for parity in range(2)
            ]
            sums = jnp.concatenate(sums, axis=1)
            deg = b * degrees + within_deg
            split = (order_size, tile, degrees)
            grad, curl = sums[:rows], sums[rows:]

            def packed(inside, sign):
                g = jnp.where(inside, sign * grad, 0.0).reshape(split)
                c = jnp.where(inside, sign * curl, 0.0).reshape(split)
                return jnp.concatenate([g, c], axis=1).astype(BF)

            out2[s, :, b] = packed(deg >= m, 1.0)
            out2[s, :, b + low] = packed(deg + low * degrees >= m, -1.0)
            return inner

        lax.fori_loop(0, low, give, 0)
        land2[s, order_pos, blk] = out2[s, order_pos, blk]
        send_all(second, s)
        return carry

    lax.fori_loop(0, group, process, 0)

    for s in range(group):
        await_all(second, s)
        got = land2[s].astype(F32).reshape(devices, 2 * tile, degrees)
        for k, ref in enumerate((grad_ref, curl_ref)):
            z = got[:, k * tile : (k + 1) * tile].reshape(devices * tile, degrees).astype(BF)
            value = turned(((0,), (0,)), z, pick[s])
            if s:
                value = value + ref[...].astype(F32)
            ref[...] = value.astype(BF)

    for s in range(group):
        sent_all(first, s)
        sent_all(second, s)


def by_realization(order_size, blk_size, emode_coeffs, lensing_coeffs, order_values, circle_indices, circle_weights):
    degrees, orders, csims = emode_coeffs.shape
    lmax = degrees * blk_size
    circle_total = circle_indices.shape[0]
    devices = order_size * blk_size
    group = csims // 2 // devices
    width = orders * csims
    tile = 2 * orders
    rows = order_size * tile

    def parted(coeffs):
        return coeffs.reshape(degrees // 2, 2, width).transpose(1, 0, 2).reshape(degrees, width)

    def joined(values):
        return values.reshape(2, degrees // 2, orders, csims).transpose(1, 0, 2, 3).reshape(degrees, orders, csims)

    dma = pltpu.SemaphoreType.DMA
    mail = pltpu.VMEM((group, order_size, blk_size, 2 * tile, degrees), BF)
    box = dma((group, order_size, blk_size))
    grad, curl = pl.pallas_call(
        functools.partial(
            realization_kernel, lmax, circle_total, order_size, blk_size, orders, csims, group
        ),
        out_shape=[jax.ShapeDtypeStruct((degrees, width), BF)] * 2,
        in_specs=[VMEM] * 5,
        out_specs=[VMEM, VMEM],
        scratch_shapes=[
            pltpu.VMEM((group, devices * tile, width), BF),
            mail, mail, mail, mail,
            pltpu.VMEM((circle_total, lmax // 2), BF),
            pltpu.VMEM((4 * rows, lmax // 2), BF),
            pltpu.VMEM((6, rows, circle_total), BF),
            pltpu.VMEM((2, 2, LONGS, rows), BF),
            pltpu.VMEM((2, rows, LONGS), BF),
            pltpu.VMEM((2, rows, circle_total), BF),
            pltpu.VMEM((2, 2 * rows, circle_total), BF),
            pltpu.VMEM((1, circle_total), F32),
            box, box, box, box,
        ],
        compiler_params=pltpu.CompilerParams(
            vmem_limit_bytes=48 << 20, collective_id=2, has_side_effects=True
        ),
        name="remap",
    )(
        parted(emode_coeffs),
        parted(lensing_coeffs),
        order_values.reshape(1, -1),
        circle_indices.reshape(-1, 128),
        circle_weights.reshape(-1, 128),
    )
    return joined(grad), joined(curl)


def splits_by_realization(order_size, blk_size, emode_coeffs, circle_indices):
    degrees, orders, csims = emode_coeffs.shape
    circle_total = circle_indices.shape[0]
    return (
        (csims // 2) % (order_size * blk_size) == 0
        and orders == 4
        and blk_size % 2 == 0
        and degrees % 256 == 0
        and degrees * blk_size == 4 * circle_total
        and circle_total % 512 == 0
    )


def body(order_size, blk_size, *arrays):
    if splits_by_realization(order_size, blk_size, arrays[0], arrays[3]):
        return by_realization(order_size, blk_size, *arrays)
    return by_circle(order_size, blk_size, *arrays)


def solution(mesh):
    in_specs = (P("blk", "order", None), P("blk", "order", None), P(), P(), P())
    out_specs = (P("blk", "order", None), P("blk", "order", None))
    sizes = (mesh.shape["order"], mesh.shape["blk"])
    return jax.shard_map(
        functools.partial(body, *sizes), mesh=mesh, in_specs=in_specs, out_specs=out_specs, check_vma=False
    )
```

```python
import functools
import math

import jax
import jax.numpy as jnp
from jax import lax
from jax.experimental import pallas as pl
from jax.experimental.pallas import tpu as pltpu
from jax.sharding import PartitionSpec as P

LONGS = 256
BF = jnp.bfloat16
F32 = jnp.float32
MESH = pl.DeviceIdType.MESH


def wrap(value, period):
    if period & (period - 1) == 0:
        return value & (period - 1)
    return jnp.mod(value, period)


def sin_cos(steps, period):
    quarter = period // 4
    steps = wrap(steps, period)
    turn = (steps + quarter // 2) // quarter if quarter & (quarter - 1) else (steps + quarter // 2) >> (quarter.bit_length() - 1)
    x = (steps - turn * quarter).astype(F32) * (2.0 * math.pi / period)
    x2 = x * x
    s = x * (1.0 + x2 * (-1.0 / 6 + x2 * (1.0 / 120 + x2 * (-1.0 / 5040 + x2 * (1.0 / 362880)))))
    c = 1.0 + x2 * (-0.5 + x2 * (1.0 / 24 + x2 * (-1.0 / 720 + x2 * (1.0 / 40320))))
    odd = (turn & 1) == 1
    sine = jnp.where(odd, c, s)
    cosine = jnp.where(odd, s, c)
    sine = jnp.where((turn & 2) == 2, -sine, sine)
    cosine = jnp.where(((turn + 1) & 2) == 2, -cosine, cosine)
    return sine, cosine


def quarter_turns(order):
    turn = order & 3
    c = jnp.where(turn == 0, 1.0, jnp.where(turn == 2, -1.0, 0.0)).astype(F32)
    s = jnp.where(turn == 1, 1.0, jnp.where(turn == 3, -1.0, 0.0)).astype(F32)
    return c, s


def neighbours(order_size, line):
    order_pos, blk = lax.axis_index("order"), lax.axis_index("blk")
    h, y = lax.div(blk, 2), lax.rem(blk, 2)
    pair = blk + 1 - 2 * y
    peers = [lax.rem(order_pos + k, order_size) for k in range(1, order_size)]
    return order_pos, blk, h, y, pair, peers


def greet(order_size, line):
    order_pos, blk, h, y, pair, peers = neighbours(order_size, line)
    barrier = pltpu.get_barrier_semaphore()

    @pl.when(h > 0)
    def _():
        pl.semaphore_signal(barrier, inc=1, device_id={"blk": blk - 2}, device_id_type=MESH)

    @pl.when(h < line - 1)
    def _():
        pl.semaphore_signal(barrier, inc=1, device_id={"blk": blk + 2}, device_id_type=MESH)

    pl.semaphore_signal(barrier, inc=1, device_id={"blk": pair}, device_id_type=MESH)
    for peer in peers:
        pl.semaphore_signal(barrier, inc=1, device_id={"order": peer}, device_id_type=MESH)
    ends = jnp.where(h > 0, 1, 0) + jnp.where(h < line - 1, 1, 0)
    pl.semaphore_wait(barrier, order_size + ends)


def remote(src, dst, send, recv, device):
    return pltpu.make_async_remote_copy(
        src_ref=src, dst_ref=dst, send_sem=send, recv_sem=recv, device_id=device, device_id_type=MESH
    )


def synth_kernel(
    lmax, circle_total, line, order_size, orders, csims,
    m_ref, r_ref, line_ref, e_ref, p_ref, out_ref,
    held, land, tab, acc, own, ysend, yrecv, asend, lens, ltab, lpart, csend, crecv,
    zs, zr, ys, yr, as_, ar, ls, lr, cs, cr,
):
    order_pos, blk, h, y, pair, peers = neighbours(order_size, line)
    rows = e_ref.shape[1]
    circles = r_ref.shape[0] // 2
    part = circles // order_size
    amplitude = math.sqrt(2.0 / lmax)
    colat = 2 * r_ref[...] + 1

    def along(src, block, o, way):
        return remote(
            src, held.at[block, o], zs.at[way, block, o], zr.at[block, o], {"blk": blk - 2 + 4 * way}
        )

    def send_own(o):
        @pl.when(h > 0)
        def _():
            along(e_ref.at[o], h, o, 0).start()

        @pl.when(h < line - 1)
        def _():
            along(e_ref.at[o], h, o, 1).start()

    def across(o):
        return remote(ysend.at[o], yrecv.at[o], ys.at[o], yr.at[o], {"blk": pair})

    def spread(o, peer, source):
        begin = pl.multiple_of(peer * part, part)
        return remote(
            asend.at[o, pl.ds(begin, part)], land.at[source * orders + o],
            as_.at[peer, o], ar.at[source, o], {"order": peer},
        )

    def share(o, lane):
        begin = pl.multiple_of(lane * rows, rows)
        return remote(
            p_ref.at[o], lens.at[o, pl.ds(begin, rows)], ls.at[o], lr.at[o], {"blk": pair}
        )

    def chain(way, target, o):
        return remote(
            csend.at[way, target, o], crecv.at[way, target, o],
            cs.at[way, target, o], cr.at[way, target, o], {"blk": blk - 2 + 4 * way},
        )

    greet(order_size, line)
    for o in range(orders):
        share(o, y).start()
        send_own(o)
    lens[:, pl.ds(pl.multiple_of(y * rows, rows), rows), :] = p_ref[...]

    def make_table(block, carry):
        degree = (2 * block + y) * rows + lax.broadcasted_iota(jnp.int32, (1, rows), 1)
        freq = 2 * degree + 1
        sine, cosine = sin_cos(colat * freq, 8 * circle_total)
        sine, cosine = sine * amplitude, cosine * amplitude
        weight = freq.astype(F32) / (2.0 * lmax)
        for k, value in enumerate((cosine, sine, cosine * weight, sine * weight)):
            tab[block, 2 * k * circles : 2 * (k + 1) * circles, :] = value.astype(BF)
        return carry

    def make_lens_table(target, carry):
        degree = 2 * h * rows + lax.broadcasted_iota(jnp.int32, (1, 2 * rows), 1)
        freq = 2 * degree + 1
        sine, cosine = sin_cos((2 * line_ref[target] + 1) * freq, 8 * circle_total)
        sine, cosine = sine * amplitude, cosine * amplitude
        weight = freq.astype(F32) / (2.0 * lmax)
        for k, value in enumerate((cosine, sine, sine * weight, cosine * weight)):
            ltab[k, target] = value.astype(BF)
        return carry

    lax.fori_loop(0, line, make_lens_table, 0)
    lax.fori_loop(0, line, make_table, 0)
    ps, pc = sin_cos(colat * 2, 8 * circle_total)
    kappa = 2.0 / (2.0 * lmax)

    def product(values, block, o):
        degree = (2 * block + y) * rows + lax.broadcasted_iota(jnp.int32, values.shape, 0)
        values = jnp.where(degree >= m_ref[o], values, jnp.zeros_like(values))
        return jnp.dot(tab[block], values, preferred_element_type=F32)

    def finish(o):
        across(o).wait_recv()
        cut = 4 * csims
        asend[o, :, :cut] = (own[o] + yrecv[o].astype(F32)).astype(BF)
        asend[o, :, cut:] = lpart[o, h].astype(BF)
        for peer in peers:
            spread(o, peer, order_pos).start()
        begin = pl.multiple_of(order_pos * part, part)
        land[order_pos * orders + o] = asend[o, pl.ds(begin, part)]

    def lens_sums(o):
        share(o, 1 - y).wait_recv()
        m = m_ref[o]
        cm, sm = quarter_turns(m)
        values = lens[o]
        degree = 2 * h * rows + lax.broadcasted_iota(jnp.int32, values.shape, 0)
        values = jnp.where(degree >= m, values, jnp.zeros_like(values))
        flat, split = (line * circles, 2 * rows), (line, circles, csims)
        theta = jnp.dot(ltab[2 + (m & 1)].reshape(flat), values, preferred_element_type=F32)
        lpart[o, :, :, :csims] = ((sm - cm) * theta).reshape(split)
        flow = jnp.dot(ltab[m & 1].reshape(flat), values, preferred_element_type=F32)
        lpart[o, :, :, csims:] = ((cm + sm) * (m.astype(F32) * (1.0 / lmax)) * flow).reshape(split)

    def stage(t, o):
        def leftward(target, carry):
            @pl.when((target <= h) & (h < line - 1))
            def _():
                chain(0, target, o).wait_recv()
                lpart[o, target] += crecv[0, target, o].astype(F32)

            @pl.when(target < h)
            def _():
                csend[0, target, o] = lpart[o, target].astype(BF)
                chain(0, target, o).start()

            return carry

        def rightward(target, carry):
            @pl.when((target >= h) & (h > 0))
            def _():
                chain(1, target, o).wait_recv()
                lpart[o, target] += crecv[1, target, o].astype(F32)

            @pl.when(target > h)
            def _():
                csend[1, target, o] = lpart[o, target].astype(BF)
                chain(1, target, o).start()

            return carry

        @pl.when(h == line - 1 - t)
        def _():
            lax.fori_loop(0, line, leftward, 0)

        @pl.when(h == t)
        def _():
            lax.fori_loop(0, line, rightward, 0)

    def hop(s, o):
        after, before = h + s, h - s

        @pl.when(after < line)
        def _():
            along(held.at[after, o], after, o, 0).wait_recv()

            @pl.when(h > 0)
            def _():
                along(held.at[after, o], after, o, 0).start()

        @pl.when(before >= 0)
        def _():
            along(held.at[before, o], before, o, 1).wait_recv()

            @pl.when(h < line - 1)
            def _():
                along(held.at[before, o], before, o, 1).start()

        @pl.when(after < line)
        def _():
            acc[o] += product(held[after, o], after, o)

        @pl.when(before >= 0)
        def _():
            acc[o] += product(held[before, o], before, o)

    def emode_maps(o):
        cm, sm = quarter_turns(m_ref[o])
        factor = m_ref[o].astype(F32) * (1.0 / lmax)
        c0, s0, gc0, gs0 = (acc[o, 2 * k * circles : 2 * (k + 1) * circles] for k in range(4))
        a, b = cm * c0 + sm * s0, cm * s0 - sm * c0
        gc, gs = cm * gc0 + sm * gs0, cm * gs0 - sm * gc0
        maps = (
            -(pc * (gs + kappa * b) + ps * (gc + kappa * a)),
            -(pc * (gs - kappa * b) - ps * (gc - kappa * a)),
            factor * (pc * a - ps * b),
            factor * (pc * a + ps * b),
        )
        for k, value in enumerate(maps):
            at = slice(k * csims, (k + 1) * csims)
            own[o, :, at] = value[:circles]
            ysend[o, :, at] = value[circles:].astype(BF)
        across(o).start()

    def one_phase(s, outer):
        def one_order(o, carry):
            @pl.when(s < line)
            def _():
                hop(s, o)

            @pl.when(s == 1)
            def _():
                lens_sums(o)

            @pl.when(s == line - 1)
            def _():
                emode_maps(o)

            stage(s - 1, o)

            @pl.when(s == line)
            def _():
                finish(o)

            return carry

        return lax.fori_loop(0, orders, one_order, outer)

    def own_product(o, carry):
        acc[o] = product(e_ref[o], h, o)
        return carry

    lax.fori_loop(0, orders, own_product, 0)
    lax.fori_loop(1, line + 1, one_phase, 0)

    def settle(o, carry):
        across(o).wait_send()
        share(o, y).wait_send()
        for peer in peers:
            spread(o, peer, order_pos).wait_send()
            spread(o, peer, peer).wait_recv()

        def sent(block, inner):
            @pl.when((h > 0) & (block >= h))
            def _():
                along(held.at[block, o], block, o, 0).wait_send()

            @pl.when((h < line - 1) & (block <= h))
            def _():
                along(held.at[block, o], block, o, 1).wait_send()

            @pl.when(block < h)
            def _():
                chain(0, block, o).wait_send()

            @pl.when(block > h)
            def _():
                chain(1, block, o).wait_send()

            return inner

        lax.fori_loop(0, line, sent, 0)
        return carry

    lax.fori_loop(0, orders, settle, 0)
    out_ref[...] = land[...]


def pixel_kernel(orders, csims, par_ref, w_ref, m_ref, f_ref, ft_ref, out_ref):
    count = m_ref.shape[0]
    sims = csims // 2
    low = lax.broadcasted_iota(jnp.int32, (orders, csims), 1) < sims
    begin = pl.program_id(0) * count

    def halves(x, y):
        first = jnp.where(low, x, pltpu.roll(y, sims, 1))
        second = jnp.where(low, pltpu.roll(x, sims, 1), y)
        return first, second

    for c in range(count):
        qt, ut, qc, uc, dt, dc = (
            m_ref[c, :, k * csims : (k + 1) * csims].astype(F32) for k in range(6)
        )
        t_re, t_im = halves(qt, ut)
        c_re, c_im = halves(qc, uc)
        dt_re, dt_im = halves(dt, dt)
        dc_re, dc_im = halves(dc, dc)
        real = jnp.concatenate([t_re, -c_im, dt_re, -dc_im], axis=1)
        imag = jnp.concatenate([t_im, c_re, dt_im, dc_re], axis=1)
        arranged = jnp.concatenate([real, imag], axis=0).astype(BF)
        parity = par_ref[begin + c]
        pixels = jnp.dot(ft_ref[parity], arranged, preferred_element_type=F32)
        deflected = (
            pixels[:, 2 * csims : 3 * csims] * pixels[:, :csims]
            + pixels[:, 3 * csims :] * pixels[:, csims : 2 * csims]
        ).astype(BF)
        analysed = jnp.dot(f_ref[parity], deflected, preferred_element_type=F32) * w_ref[begin + c]
        gq, gu = halves(analysed[:orders], analysed[orders:])
        out_ref[c, :, :csims] = gq.astype(BF)
        out_ref[c, :, csims:] = gu.astype(BF)


def adjoint_kernel(
    lmax, circle_total, line, order_size, orders, csims,
    m_ref, r_ref, rc_ref, w_ref, grad_ref, curl_ref,
    gath, tab, acc, zs, zr, ys, yr, as_, ar,
):
    order_pos, blk, h, y, pair, peers = neighbours(order_size, line)
    degrees = grad_ref.shape[0]
    circles = gath.shape[2]
    part = w_ref.shape[1]
    amplitude = math.sqrt(2.0 / lmax)

    def back(peer, source):
        begin = pl.multiple_of(source * part, part)
        return remote(
            w_ref.at[pl.ds(peer * orders, orders)], gath.at[blk, :, pl.ds(begin, part)],
            as_.at[peer], ar.at[source], {"order": peer},
        )

    def along(line_at, way):
        block = gath.at[2 * line_at + y]
        return remote(block, block, zs.at[way, line_at], zr.at[line_at], {"blk": blk - 2 + 4 * way})

    def across(line_at, lane):
        block = gath.at[2 * line_at + lane]
        return remote(block, block, ys.at[line_at], yr.at[line_at], {"blk": pair})

    greet(order_size, line)
    for peer in peers:
        back(peer, order_pos).start()
    begin = pl.multiple_of(order_pos * part, part)
    gath[blk, :, pl.ds(begin, part), :] = w_ref[pl.ds(order_pos * orders, orders)]

    def make_table(block, carry):
        degree = blk * degrees + lax.broadcasted_iota(jnp.int32, (degrees, 1), 0)
        sine, cosine = sin_cos((2 * degree + 1) * (2 * r_ref[block] + 1), 8 * circle_total)
        tab[block, :, :circles] = (cosine * amplitude).astype(BF)
        tab[block, :, circles:] = (sine * amplitude).astype(BF)
        return carry

    lax.fori_loop(0, line // 2, make_table, 0)

    def add(block):
        ps, pc = sin_cos(2 * (2 * rc_ref[block] + 1), 8 * circle_total)
        ups, vps = [], []
        for o in range(orders):
            cm, sm = quarter_turns(m_ref[o])
            gq = gath[block, o, :, :csims].astype(F32)
            gu = gath[block, o, :, csims:].astype(F32)
            x1, y1 = pc * (gq + gu), ps * (gq - gu)
            x2, y2 = pc * (gu - gq), ps * (gu + gq)
            ups += [(cm * x1 + sm * y1).astype(BF), (cm * x2 + sm * y2).astype(BF)]
            vps += [(sm * x1 - cm * y1).astype(BF), (sm * x2 - cm * y2).astype(BF)]
        values = jnp.concatenate(
            [jnp.concatenate(ups, axis=1), jnp.concatenate(vps, axis=1)], axis=0
        )
        acc[...] += jnp.dot(tab[block], values, preferred_element_type=F32)

    for peer in peers:
        back(peer, peer).wait_recv()

    @pl.when(h > 0)
    def _():
        along(h, 0).start()

    @pl.when(h < line - 1)
    def _():
        along(h, 1).start()

    across(h, y).start()
    lax.fori_loop(line // 2, 2 * line, make_table, 0)
    acc[...] = jnp.zeros_like(acc)

    def hop(s, carry):
        after, before = h + s, h - s

        @pl.when((s > 0) & (after < line))
        def _():
            along(after, 0).wait_recv()

            @pl.when(h > 0)
            def _():
                along(after, 0).start()

            across(after, y).start()

        @pl.when((s > 0) & (before >= 0))
        def _():
            along(before, 1).wait_recv()

            @pl.when(h < line - 1)
            def _():
                along(before, 1).start()

            across(before, y).start()

        @pl.when(after < line)
        def _():
            add(2 * after + y)

        @pl.when((s > 0) & (before >= 0))
        def _():
            add(2 * before + y)

        return carry

    lax.fori_loop(0, line, hop, 0)

    def cross(s, carry):
        after, before = h + s, h - s

        @pl.when(after < line)
        def _():
            across(after, 1 - y).wait_recv()
            add(2 * after + 1 - y)

        @pl.when((s > 0) & (before >= 0))
        def _():
            across(before, 1 - y).wait_recv()
            add(2 * before + 1 - y)

        return carry

    lax.fori_loop(0, line, cross, 0)
    for peer in peers:
        back(peer, order_pos).wait_send()

    def settle(line_at, carry):
        across(line_at, y).wait_send()

        @pl.when((h > 0) & (line_at >= h))
        def _():
            along(line_at, 0).wait_send()

        @pl.when((h < line - 1) & (line_at <= h))
        def _():
            along(line_at, 1).wait_send()

        return carry

    lax.fori_loop(0, line, settle, 0)
    rows = blk * degrees + lax.broadcasted_iota(jnp.int32, (degrees, csims), 0)
    for o in range(orders):
        inside = rows >= m_ref[o]
        at = slice(o * csims, (o + 1) * csims)
        grad = acc[:, 2 * o * csims : (2 * o + 1) * csims]
        curl = acc[:, (2 * o + 1) * csims : (2 * o + 2) * csims]
        grad_ref[:, at] = jnp.where(inside, grad, 0.0).astype(BF)
        curl_ref[:, at] = jnp.where(inside, curl, 0.0).astype(BF)


def longitude_table(lmax, parity, order_list):
    full_circle = 2 * lmax
    longitude = jnp.arange(LONGS, dtype=jnp.int32)
    phase_steps = order_list[None, :, None] * (2 * longitude[None, None, :] + parity[:, None, None])
    phase_steps = jnp.mod(phase_steps, 2 * full_circle)
    angles = phase_steps.astype(jnp.float32) * (math.pi / full_circle)
    scaling = 1.0 / math.sqrt(order_list.shape[0])
    fourier = jnp.concatenate([jnp.cos(angles) * scaling, -jnp.sin(angles) * scaling], axis=1)
    return fourier.astype(BF)


def divisor(total, limit):
    return next(k for k in range(min(total, limit), 0, -1) if total % k == 0)


SMEM = pl.BlockSpec(memory_space=pltpu.SMEM)
VMEM = pl.BlockSpec(memory_space=pltpu.VMEM)
PARAMS = pltpu.CompilerParams(vmem_limit_bytes=48 << 20)


def by_circle(order_size, blk_size, emode_coeffs, lensing_coeffs, order_values, circle_indices, circle_weights):
    degree_local, orders, csims = emode_coeffs.shape
    lmax = degree_local * blk_size
    circle_total = circle_indices.shape[0]
    order_total = order_values.shape[0]
    circles = circle_total // blk_size
    order_pos = lax.axis_index("order")
    block_pos = lax.axis_index("blk")
    my_orders = lax.dynamic_slice_in_dim(order_values, order_pos * orders, orders)
    width = orders * csims
    line = blk_size // 2
    blocks = circle_indices.reshape(blk_size, circles)
    pair_circles = jnp.concatenate(
        [
            lax.dynamic_index_in_dim(blocks, block_pos, 0, keepdims=False),
            lax.dynamic_index_in_dim(blocks, block_pos ^ 1, 0, keepdims=False),
        ]
    )
    line_circles = lax.dynamic_index_in_dim(
        circle_indices.reshape(line, 2, circles), block_pos % 2, 1, keepdims=False
    )
    fourier = longitude_table(lmax, jnp.arange(2, dtype=jnp.int32), order_values)
    fourier_t = fourier.transpose(0, 2, 1)
    part = circles // order_size
    dma = pltpu.SemaphoreType.DMA
    spread = pl.pallas_call(
        functools.partial(synth_kernel, lmax, circle_total, line, order_size, orders, csims),
        out_shape=jax.ShapeDtypeStruct((order_total, part, 6 * csims), BF),
        in_specs=[SMEM, VMEM, VMEM, VMEM, VMEM],
        out_specs=VMEM,
        scratch_shapes=[
            pltpu.VMEM((line, orders, degree_local, csims), BF),
            pltpu.VMEM((order_total, part, 6 * csims), BF),
            pltpu.VMEM((line, 8 * circles, degree_local), BF),
            pltpu.VMEM((orders, 8 * circles, csims), F32),
            pltpu.VMEM((orders, circles, 4 * csims), F32),
            pltpu.VMEM((orders, circles, 4 * csims), BF),
            pltpu.VMEM((orders, circles, 4 * csims), BF),
            pltpu.VMEM((orders, circles, 6 * csims), BF),
            pltpu.VMEM((orders, 2 * degree_local, csims), BF),
            pltpu.VMEM((4, line, circles, 2 * degree_local), BF),
            pltpu.VMEM((orders, line, circles, 2 * csims), F32),
            pltpu.VMEM((2, line, orders, circles, 2 * csims), BF),
            pltpu.VMEM((2, line, orders, circles, 2 * csims), BF),
            dma((2, line, orders)),
            dma((line, orders)),
            dma((orders,)),
            dma((orders,)),
            dma((order_size, orders)),
            dma((order_size, orders)),
            dma((orders,)),
            dma((orders,)),
            dma((2, line, orders)),
            dma((2, line, orders)),
        ],
        compiler_params=pltpu.CompilerParams(
            vmem_limit_bytes=48 << 20, collective_id=0, has_side_effects=True
        ),
        name="synth",
    )(
        my_orders,
        pair_circles[:, None],
        line_circles[:, :, None],
        emode_coeffs.transpose(1, 0, 2),
        lensing_coeffs.transpose(1, 0, 2),
    )
    spread = spread.transpose(1, 0, 2)
    begin = block_pos * circles + order_pos * part
    part_circles = lax.dynamic_slice_in_dim(circle_indices, begin, part)
    part_weights = lax.dynamic_slice_in_dim(circle_weights, begin, part)
    count = divisor(part, 8)
    weighted = pl.pallas_call(
        functools.partial(pixel_kernel, order_total, csims),
        out_shape=jax.ShapeDtypeStruct((part, order_total, 2 * csims), BF),
        grid=(part // count,),
        in_specs=[
            SMEM,
            SMEM,
            pl.BlockSpec((count, order_total, 6 * csims), lambda i: (i, 0, 0)),
            pl.BlockSpec((2, 2 * order_total, LONGS), lambda i: (0, 0, 0)),
            pl.BlockSpec((2, LONGS, 2 * order_total), lambda i: (0, 0, 0)),
        ],
        out_specs=pl.BlockSpec((count, order_total, 2 * csims), lambda i: (i, 0, 0)),
        compiler_params=PARAMS,
        name="pixels",
    )(jnp.mod(part_circles, 2), part_weights, spread, fourier, fourier_t)
    grad, curl = pl.pallas_call(
        functools.partial(adjoint_kernel, lmax, circle_total, line, order_size, orders, csims),
        out_shape=[jax.ShapeDtypeStruct((degree_local, width), BF)] * 2,
        in_specs=[SMEM, VMEM, VMEM, VMEM],
        out_specs=[VMEM, VMEM],
        scratch_shapes=[
            pltpu.VMEM((blk_size, orders, circles, 2 * csims), BF),
            pltpu.VMEM((blk_size, degree_local, 2 * circles), BF),
            pltpu.VMEM((degree_local, 2 * width), F32),
            dma((2, line)),
            dma((line,)),
            dma((line,)),
            dma((line,)),
            dma((order_size,)),
            dma((order_size,)),
        ],
        compiler_params=pltpu.CompilerParams(
            vmem_limit_bytes=48 << 20, collective_id=1, has_side_effects=True
        ),
        name="adjoint",
    )(my_orders, blocks[:, None, :], blocks[:, :, None], weighted.transpose(1, 0, 2))
    return grad.reshape(emode_coeffs.shape), curl.reshape(emode_coeffs.shape)


def turned(dims, left, right):
    return lax.dot_general(left, right, (dims, ((), ())), preferred_element_type=F32)


def realization_kernel(
    lmax, circle_total, order_size, blk_size, orders, csims, group,
    em_ref, le_ref, m_any, ci_any, cw_any, grad_ref, curl_ref,
    raw, wide, flat_in, m_ref, ci_ref, cw_ref,
    pick, out1, land1, out2, land2, tab, xs, maps, waves, waves_t, ana, pairs, wlane,
    s1, r1, s2, r2, pull,
):
    order_pos, blk = lax.axis_index("order"), lax.axis_index("blk")
    devices = order_size * blk_size
    me = order_pos * blk_size + blk
    degrees = em_ref.shape[0] // orders
    half = degrees // 2
    sims = csims // 2
    low = blk_size // 2
    span = low * half
    couples = circle_total // 2
    quarter = couples // 2
    rows = order_size * 2 * orders
    tile = 2 * orders
    full = 8 * circle_total
    width = orders * csims

    pulls = [
        pltpu.make_async_copy(src, dst, pull.at[k])
        for k, (src, dst) in enumerate(
            ((em_ref, raw.at[0]), (le_ref, raw.at[1]), (m_any, m_ref), (ci_any, ci_ref), (cw_any, cw_ref))
        )
    ]
    for copy in pulls:
        copy.start()

    late_from = blk_size - blk_size // 4
    early = blk < late_from
    early_total = order_size * late_from
    late_total = devices - early_total

    def each(begin, end, act):
        def one(k, carry):
            b = begin + lax.div(k, order_size)
            o = lax.rem(order_pos + lax.rem(k, order_size), order_size)

            @pl.when((o != order_pos) | (b != blk))
            def _():
                act(o, b)

            return carry

        lax.fori_loop(0, (end - begin) * order_size, one, 0)

    def hand(src, dst, send, recv, s, o, b):
        return pltpu.make_async_remote_copy(
            src_ref=src.at[s, o, b], dst_ref=dst.at[s, order_pos, blk],
            send_sem=send.at[s, o, b], recv_sem=recv.at[s, order_pos, blk],
            device_id={"order": o, "blk": b}, device_id_type=MESH,
        )

    def arrival(src, dst, send, recv, s, o, b):
        return pltpu.make_async_remote_copy(
            src_ref=src.at[s, o, b], dst_ref=dst.at[s, o, b],
            send_sem=send.at[s, o, b], recv_sem=recv.at[s, o, b],
            device_id={"order": o, "blk": b}, device_id_type=MESH,
        )

    first = (out1, land1, s1, r1)
    second = (out2, land2, s2, r2)

    def send_to(args, s, begin, end):
        each(begin, end, lambda o, b: hand(*args, s, o, b).start())

    def send_all(args, s):
        each(0, blk_size, lambda o, b: hand(*args, s, o, b).start())

    def await_all(args, s):
        each(0, blk_size, lambda o, b: arrival(*args, s, o, b).wait_recv())

    def sent_all(args, s):
        each(0, blk_size, lambda o, b: hand(*args, s, o, b).wait_send())

    barrier = pltpu.get_barrier_semaphore()

    def hail(begin, end):
        each(
            begin, end,
            lambda o, b: pl.semaphore_signal(
                barrier, inc=1, device_id={"order": o, "blk": b}, device_id_type=MESH
            ),
        )

    @pl.when(early)
    def _():
        hail(0, late_from)

    @pl.when(jnp.logical_not(early))
    def _():
        hail(late_from, blk_size)

    def strands():
        for o in range(orders):
            for parity in range(2):
                yield (
                    pl.ds(o + orders * parity, half, stride=2 * orders),
                    slice(parity * half, (parity + 1) * half), slice(o * csims, (o + 1) * csims),
                )

    def unpack(k):
        pulls[k].wait()
        wide[k] = raw[k].astype(F32)
        for mixed, rows_at, lanes_at in strands():
            flat_in[k, rows_at, lanes_at] = wide[k, mixed, :].astype(BF)

    def choose(s):
        row = lax.broadcasted_iota(jnp.int32, (devices * tile, 1), 0)
        within = lax.rem(row, tile)
        column = (
            lax.rem(within, orders) * csims + lax.div(within, orders) * sims + lax.div(row, tile) * group + s
        )
        lane = lax.broadcasted_iota(jnp.int32, (devices * tile, width), 1)
        choice = jnp.where(lane == column, 1.0, 0.0).astype(BF)
        pick[s] = choice

    def arrange(s):
        split = (devices, tile, degrees)
        e = turned(((1,), (1,)), pick[s], flat_in[0]).reshape(split)
        p = turned(((1,), (1,)), pick[s], flat_in[1]).reshape(split)
        both = jnp.concatenate([e, p], axis=1).astype(BF)
        out1[s] = both.reshape(order_size, blk_size, 2 * tile, degrees)
        land1[s, order_pos, blk] = out1[s, order_pos, blk]

    choose(0)
    for k in range(2):
        unpack(k)
    arrange(0)

    @pl.when(early)
    def _():
        pl.semaphore_wait(barrier, early_total - 1)
        hail(late_from, blk_size)
        send_to(first, 0, 0, late_from)

    @pl.when(jnp.logical_not(early))
    def _():
        pl.semaphore_wait(barrier, devices - 1)
        hail(0, late_from)
        send_to(first, 0, 0, blk_size)

    for s in range(1, group):
        choose(s)
        arrange(s)

    @pl.when(early)
    def _():
        pl.semaphore_wait(barrier, late_total)
        send_to(first, 0, late_from, blk_size)

    for s in range(1, group):
        send_all(first, s)

    for copy in pulls[2:]:
        copy.wait()
    amplitude = math.sqrt(2.0 / lmax)
    chunk = 64

    def make_table(i, carry):
        begin = pl.multiple_of(i * chunk, chunk)
        q = i * chunk + lax.broadcasted_iota(jnp.int32, (chunk, 1), 0)
        colat = 2 * (2 * lax.rem(q, quarter) + lax.div(q, quarter)) + 1
        step = 4 * lax.broadcasted_iota(jnp.int32, (1, half), 1)
        sb, cb = sin_cos(colat * step, full)
        k = lax.broadcasted_iota(jnp.int32, (1, 128), 1)
        start = 2 * degrees * lax.rem(k, low) + 2 * lax.div(k, low) + 1
        sa, ca = sin_cos(colat * start, full)
        sa, ca = sa * amplitude, ca * amplitude
        for n in range(2 * low):
            at = slice(n * half, (n + 1) * half)
            s0, c0 = sa[:, n : n + 1], ca[:, n : n + 1]
            tab[pl.ds(begin, chunk), at] = (c0 * cb - s0 * sb).astype(BF)
            tab[pl.ds(couples + begin, chunk), at] = (s0 * cb + c0 * sb).astype(BF)
        return carry

    lax.fori_loop(0, couples // chunk, make_table, 0)

    row = lax.broadcasted_iota(jnp.int32, (rows, 1), 0)
    slot = lax.div(row, tile) * orders + lax.rem(row, orders)
    imaginary = lax.rem(lax.div(row, orders), 2) == 1
    order_total = m_ref.shape[1]
    slots = lax.broadcasted_iota(jnp.int32, (rows, order_total), 1)
    m = jnp.sum(
        jnp.where(slots == slot, m_ref[...].astype(F32), 0.0), axis=1, keepdims=True
    ).astype(jnp.int32)
    cm, sm = quarter_turns(m)
    factor = m.astype(F32) * (1.0 / lmax)

    lane = lax.broadcasted_iota(jnp.int32, (1, circle_total), 1)
    at_couple = lax.rem(lane, couples)
    near = 2 * lax.rem(at_couple, quarter) + lax.div(at_couple, quarter)
    circle = jnp.where(lane < couples, near, circle_total - 1 - near)
    ps, pc = sin_cos(2 * (2 * circle + 1), full)

    index_t = ci_ref[...].astype(F32).T
    weight_t = cw_ref[...].T
    circle_f = circle.astype(F32)
    total = jnp.zeros((8, circle_total), F32)
    for k in range(ci_ref.shape[0]):
        for g in range(ci_ref.shape[1] // 8):
            at = slice(8 * g, 8 * g + 8)
            total += jnp.where(index_t[at, k : k + 1] == circle_f, weight_t[at, k : k + 1], 0.0)
    wlane[...] = jnp.sum(total, axis=0, keepdims=True)

    scaling = 1.0 / math.sqrt(order_total)
    turn = 2 * lmax
    longitude = lax.broadcasted_iota(jnp.int32, (1, LONGS), 1)
    for parity in range(2):
        si, co = sin_cos(m * (2 * longitude + parity), 2 * turn)
        si, co = si * scaling, co * scaling
        straight = jnp.where(imaginary, -si, co)
        crossed = jnp.where(imaginary, -co, -si)
        waves_t[parity] = straight.astype(BF)
        waves[parity, 0] = straight.T.astype(BF)
        waves[parity, 1] = crossed.T.astype(BF)

    kappa = 2.0 / (2.0 * lmax)
    within_deg = lax.broadcasted_iota(jnp.int32, (1, degrees), 1)
    within_deg = 2 * lax.rem(within_deg, half) + lax.div(within_deg, half)

    def process(s, carry):
        await_all(first, s)

        def fold(b, inner):
            deg = b * degrees + within_deg
            far = deg + low * degrees
            wd = (2 * deg + 1).astype(F32) * (1.0 / (2.0 * lmax))
            wf = (2 * far + 1).astype(F32) * (1.0 / (2.0 * lmax))
            one, two = land1[s, :, b].astype(F32), land1[s, :, b + low].astype(F32)
            for k in range(2):
                x = one[:, k * tile : (k + 1) * tile].reshape(rows, degrees)
                z = two[:, k * tile : (k + 1) * tile].reshape(rows, degrees)
                x = jnp.where(deg >= m, x, 0.0)
                z = jnp.where(far >= m, z, 0.0)
                flat, steep = (x - z).astype(BF), (wd * x - wf * z).astype(BF)
                for parity in range(2):
                    to = pl.ds(pl.multiple_of(parity * span + b * half, half), half)
                    of = slice(parity * half, (parity + 1) * half)
                    xs[2 * k * rows : (2 * k + 1) * rows, to] = flat[:, of]
                    xs[(2 * k + 1) * rows : (2 * k + 2) * rows, to] = steep[:, of]
            return inner

        lax.fori_loop(0, low, fold, 0)
        even = turned(((1,), (1,)), xs[:, :span], tab[:, :span])
        odd = turned(((1,), (1,)), xs[:, span:], tab[:, span:])
        plus, minus = even + odd, even - odd
        c_all = jnp.concatenate([plus[:, :couples], minus[:, couples:]], axis=1)
        s_all = jnp.concatenate([plus[:, couples:], minus[:, :couples]], axis=1)

        def turns(k):
            at = slice(k * rows, (k + 1) * rows)
            c0, s0 = c_all[at], s_all[at]
            return cm * c0 + sm * s0, cm * s0 - sm * c0

        a, b = turns(0)
        gc, gs = turns(1)
        la, _ = turns(2)
        _, lgs = turns(3)
        maps[0] = (-(pc * (gs + kappa * b) + ps * (gc + kappa * a))).astype(BF)
        maps[1] = (-(pc * (gs - kappa * b) - ps * (gc - kappa * a))).astype(BF)
        maps[2] = (-lgs).astype(BF)
        maps[3] = (factor * (pc * a - ps * b)).astype(BF)
        maps[4] = (factor * (pc * a + ps * b)).astype(BF)
        maps[5] = (factor * la).astype(BF)

        def pixels(n, inner):
            at = pl.ds(pl.multiple_of(n * quarter, quarter), quarter)
            parity = lax.rem(n + lax.div(n, 2), 2)
            qt, ut, dt = (
                jnp.dot(waves[parity, 0], maps[k, :, at], preferred_element_type=F32) for k in range(3)
            )
            qp, up, dp = (
                jnp.dot(waves[parity, 1], maps[k, :, at], preferred_element_type=F32) for k in range(3, 6)
            )
            dq = (dt * qt + dp * qp).astype(BF)
            du = (dt * ut + dp * up).astype(BF)
            w = wlane[:, at]
            ana[0, :, at] = (jnp.dot(waves_t[parity], dq, preferred_element_type=F32) * w).astype(BF)
            ana[1, :, at] = (jnp.dot(waves_t[parity], du, preferred_element_type=F32) * w).astype(BF)
            return inner

        lax.fori_loop(0, 4, pixels, 0)
        gq, gu = ana[0].astype(F32), ana[1].astype(F32)
        x1, y1 = pc * (gq + gu), ps * (gq - gu)
        x2, y2 = pc * (gu - gq), ps * (gu + gq)
        for k, (x, y) in enumerate(((x1, y1), (x2, y2))):
            at = slice(k * rows, (k + 1) * rows)
            up, vp = cm * x + sm * y, sm * x - cm * y
            near_u, far_u = up[:, :couples], up[:, couples:]
            near_v, far_v = vp[:, :couples], vp[:, couples:]
            pairs[0, at, :couples] = (near_u + far_v).astype(BF)
            pairs[0, at, couples:] = (near_v + far_u).astype(BF)
            pairs[1, at, :couples] = (near_u - far_v).astype(BF)
            pairs[1, at, couples:] = (near_v - far_u).astype(BF)

        def give(b, inner):
            sums = [
                jnp.dot(
                    pairs[parity],
                    tab[:, pl.ds(pl.multiple_of(parity * span + b * half, half), half)],
                    preferred_element_type=F32,
                )
                for parity in range(2)
            ]
            sums = jnp.concatenate(sums, axis=1)
            deg = b * degrees + within_deg
            split = (order_size, tile, degrees)
            grad, curl = sums[:rows], sums[rows:]

            def packed(inside, sign):
                g = jnp.where(inside, sign * grad, 0.0).reshape(split)
                c = jnp.where(inside, sign * curl, 0.0).reshape(split)
                return jnp.concatenate([g, c], axis=1).astype(BF)

            out2[s, :, b] = packed(deg >= m, 1.0)
            out2[s, :, b + low] = packed(deg + low * degrees >= m, -1.0)
            return inner

        lax.fori_loop(0, low, give, 0)
        land2[s, order_pos, blk] = out2[s, order_pos, blk]
        send_all(second, s)
        return carry

    lax.fori_loop(0, group, process, 0)

    for s in range(group):
        await_all(second, s)
        got = land2[s].astype(F32).reshape(devices, 2 * tile, degrees)
        for k, ref in enumerate((grad_ref, curl_ref)):
            z = got[:, k * tile : (k + 1) * tile].reshape(devices * tile, degrees).astype(BF)
            value = turned(((0,), (0,)), z, pick[s])
            for mixed, rows_at, lanes_at in strands():
                part = value[rows_at, lanes_at]
                if s:
                    part = part + wide[k, mixed, :]
                wide[k, mixed, :] = part
            if s == group - 1:
                ref[...] = wide[k].astype(BF)

    for s in range(group):
        sent_all(first, s)
        sent_all(second, s)


def by_realization(order_size, blk_size, emode_coeffs, lensing_coeffs, order_values, circle_indices, circle_weights):
    degrees, orders, csims = emode_coeffs.shape
    lmax = degrees * blk_size
    circle_total = circle_indices.shape[0]
    devices = order_size * blk_size
    group = csims // 2 // devices
    width = orders * csims
    tile = 2 * orders
    rows = order_size * tile

    dma = pltpu.SemaphoreType.DMA
    mail = pltpu.VMEM((group, order_size, blk_size, 2 * tile, degrees), BF)
    box = dma((group, order_size, blk_size))
    grad, curl = pl.pallas_call(
        functools.partial(
            realization_kernel, lmax, circle_total, order_size, blk_size, orders, csims, group
        ),
        out_shape=[jax.ShapeDtypeStruct((degrees * orders, csims), BF)] * 2,
        in_specs=[pl.BlockSpec(memory_space=pl.ANY)] * 5,
        out_specs=[VMEM, VMEM],
        scratch_shapes=[
            pltpu.VMEM((2, degrees * orders, csims), BF),
            pltpu.VMEM((2, degrees * orders, csims), F32),
            pltpu.VMEM((2, degrees, width), BF),
            pltpu.VMEM((1, order_values.shape[0]), jnp.int32),
            pltpu.VMEM((circle_total // 128, 128), jnp.int32),
            pltpu.VMEM((circle_total // 128, 128), F32),
            pltpu.VMEM((group, devices * tile, width), BF),
            mail, mail, mail, mail,
            pltpu.VMEM((circle_total, lmax // 2), BF),
            pltpu.VMEM((4 * rows, lmax // 2), BF),
            pltpu.VMEM((6, rows, circle_total), BF),
            pltpu.VMEM((2, 2, LONGS, rows), BF),
            pltpu.VMEM((2, rows, LONGS), BF),
            pltpu.VMEM((2, rows, circle_total), BF),
            pltpu.VMEM((2, 2 * rows, circle_total), BF),
            pltpu.VMEM((1, circle_total), F32),
            box, box, box, box,
            dma((5,)),
        ],
        compiler_params=pltpu.CompilerParams(
            vmem_limit_bytes=55200000, collective_id=2, has_side_effects=True
        ),
        name="remap",
    )(
        emode_coeffs.reshape(degrees * orders, csims),
        lensing_coeffs.reshape(degrees * orders, csims),
        order_values.reshape(1, -1),
        circle_indices.reshape(-1, 128),
        circle_weights.reshape(-1, 128),
    )
    return grad.reshape(emode_coeffs.shape), curl.reshape(emode_coeffs.shape)


def splits_by_realization(order_size, blk_size, emode_coeffs, circle_indices):
    degrees, orders, csims = emode_coeffs.shape
    circle_total = circle_indices.shape[0]
    return (
        (csims // 2) % (order_size * blk_size) == 0
        and orders == 4
        and blk_size % 2 == 0
        and degrees % 256 == 0
        and degrees * blk_size == 4 * circle_total
        and circle_total % 512 == 0
    )


def body(order_size, blk_size, *arrays):
    if splits_by_realization(order_size, blk_size, arrays[0], arrays[3]):
        return by_realization(order_size, blk_size, *arrays)
    return by_circle(order_size, blk_size, *arrays)


def solution(mesh):
    in_specs = (P("blk", "order", None), P("blk", "order", None), P(), P(), P())
    out_specs = (P("blk", "order", None), P("blk", "order", None))
    sizes = (mesh.shape["order"], mesh.shape["blk"])
    return jax.shard_map(
        functools.partial(body, *sizes), mesh=mesh, in_specs=in_specs, out_specs=out_specs, check_vma=False
    )
```

```python
import functools
import math

import jax
import jax.numpy as jnp
from jax import lax
from jax.experimental import pallas as pl
from jax.experimental.pallas import tpu as pltpu
from jax.sharding import PartitionSpec as P

LONGS = 256
BF = jnp.bfloat16
F32 = jnp.float32
MESH = pl.DeviceIdType.MESH


def wrap(value, period):
    if period & (period - 1) == 0:
        return value & (period - 1)
    return jnp.mod(value, period)


def sin_cos(steps, period):
    quarter = period // 4
    steps = wrap(steps, period)
    turn = (steps + quarter // 2) // quarter if quarter & (quarter - 1) else (steps + quarter // 2) >> (quarter.bit_length() - 1)
    x = (steps - turn * quarter).astype(F32) * (2.0 * math.pi / period)
    x2 = x * x
    s = x * (1.0 + x2 * (-1.0 / 6 + x2 * (1.0 / 120 + x2 * (-1.0 / 5040 + x2 * (1.0 / 362880)))))
    c = 1.0 + x2 * (-0.5 + x2 * (1.0 / 24 + x2 * (-1.0 / 720 + x2 * (1.0 / 40320))))
    odd = (turn & 1) == 1
    sine = jnp.where(odd, c, s)
    cosine = jnp.where(odd, s, c)
    sine = jnp.where((turn & 2) == 2, -sine, sine)
    cosine = jnp.where(((turn + 1) & 2) == 2, -cosine, cosine)
    return sine, cosine


def quarter_turns(order):
    turn = order & 3
    c = jnp.where(turn == 0, 1.0, jnp.where(turn == 2, -1.0, 0.0)).astype(F32)
    s = jnp.where(turn == 1, 1.0, jnp.where(turn == 3, -1.0, 0.0)).astype(F32)
    return c, s


def neighbours(order_size, line):
    order_pos, blk = lax.axis_index("order"), lax.axis_index("blk")
    h, y = lax.div(blk, 2), lax.rem(blk, 2)
    pair = blk + 1 - 2 * y
    peers = [lax.rem(order_pos + k, order_size) for k in range(1, order_size)]
    return order_pos, blk, h, y, pair, peers


def greet(order_size, line):
    order_pos, blk, h, y, pair, peers = neighbours(order_size, line)
    barrier = pltpu.get_barrier_semaphore()

    @pl.when(h > 0)
    def _():
        pl.semaphore_signal(barrier, inc=1, device_id={"blk": blk - 2}, device_id_type=MESH)

    @pl.when(h < line - 1)
    def _():
        pl.semaphore_signal(barrier, inc=1, device_id={"blk": blk + 2}, device_id_type=MESH)

    pl.semaphore_signal(barrier, inc=1, device_id={"blk": pair}, device_id_type=MESH)
    for peer in peers:
        pl.semaphore_signal(barrier, inc=1, device_id={"order": peer}, device_id_type=MESH)
    ends = jnp.where(h > 0, 1, 0) + jnp.where(h < line - 1, 1, 0)
    pl.semaphore_wait(barrier, order_size + ends)


def remote(src, dst, send, recv, device):
    return pltpu.make_async_remote_copy(
        src_ref=src, dst_ref=dst, send_sem=send, recv_sem=recv, device_id=device, device_id_type=MESH
    )


def synth_kernel(
    lmax, circle_total, line, order_size, orders, csims,
    m_ref, r_ref, line_ref, e_ref, p_ref, out_ref,
    held, land, tab, acc, own, ysend, yrecv, asend, lens, ltab, lpart, csend, crecv,
    zs, zr, ys, yr, as_, ar, ls, lr, cs, cr,
):
    order_pos, blk, h, y, pair, peers = neighbours(order_size, line)
    rows = e_ref.shape[1]
    circles = r_ref.shape[0] // 2
    part = circles // order_size
    amplitude = math.sqrt(2.0 / lmax)
    colat = 2 * r_ref[...] + 1

    def along(src, block, o, way):
        return remote(
            src, held.at[block, o], zs.at[way, block, o], zr.at[block, o], {"blk": blk - 2 + 4 * way}
        )

    def send_own(o):
        @pl.when(h > 0)
        def _():
            along(e_ref.at[o], h, o, 0).start()

        @pl.when(h < line - 1)
        def _():
            along(e_ref.at[o], h, o, 1).start()

    def across(o):
        return remote(ysend.at[o], yrecv.at[o], ys.at[o], yr.at[o], {"blk": pair})

    def spread(o, peer, source):
        begin = pl.multiple_of(peer * part, part)
        return remote(
            asend.at[o, pl.ds(begin, part)], land.at[source * orders + o],
            as_.at[peer, o], ar.at[source, o], {"order": peer},
        )

    def share(o, lane):
        begin = pl.multiple_of(lane * rows, rows)
        return remote(
            p_ref.at[o], lens.at[o, pl.ds(begin, rows)], ls.at[o], lr.at[o], {"blk": pair}
        )

    def chain(way, target, o):
        return remote(
            csend.at[way, target, o], crecv.at[way, target, o],
            cs.at[way, target, o], cr.at[way, target, o], {"blk": blk - 2 + 4 * way},
        )

    greet(order_size, line)
    for o in range(orders):
        share(o, y).start()
        send_own(o)
    lens[:, pl.ds(pl.multiple_of(y * rows, rows), rows), :] = p_ref[...]

    def make_table(block, carry):
        degree = (2 * block + y) * rows + lax.broadcasted_iota(jnp.int32, (1, rows), 1)
        freq = 2 * degree + 1
        sine, cosine = sin_cos(colat * freq, 8 * circle_total)
        sine, cosine = sine * amplitude, cosine * amplitude
        weight = freq.astype(F32) / (2.0 * lmax)
        for k, value in enumerate((cosine, sine, cosine * weight, sine * weight)):
            tab[block, 2 * k * circles : 2 * (k + 1) * circles, :] = value.astype(BF)
        return carry

    def make_lens_table(target, carry):
        degree = 2 * h * rows + lax.broadcasted_iota(jnp.int32, (1, 2 * rows), 1)
        freq = 2 * degree + 1
        sine, cosine = sin_cos((2 * line_ref[target] + 1) * freq, 8 * circle_total)
        sine, cosine = sine * amplitude, cosine * amplitude
        weight = freq.astype(F32) / (2.0 * lmax)
        for k, value in enumerate((cosine, sine, sine * weight, cosine * weight)):
            ltab[k, target] = value.astype(BF)
        return carry

    lax.fori_loop(0, line, make_lens_table, 0)
    lax.fori_loop(0, line, make_table, 0)
    ps, pc = sin_cos(colat * 2, 8 * circle_total)
    kappa = 2.0 / (2.0 * lmax)

    def product(values, block, o):
        degree = (2 * block + y) * rows + lax.broadcasted_iota(jnp.int32, values.shape, 0)
        values = jnp.where(degree >= m_ref[o], values, jnp.zeros_like(values))
        return jnp.dot(tab[block], values, preferred_element_type=F32)

    def finish(o):
        across(o).wait_recv()
        cut = 4 * csims
        asend[o, :, :cut] = (own[o] + yrecv[o].astype(F32)).astype(BF)
        asend[o, :, cut:] = lpart[o, h].astype(BF)
        for peer in peers:
            spread(o, peer, order_pos).start()
        begin = pl.multiple_of(order_pos * part, part)
        land[order_pos * orders + o] = asend[o, pl.ds(begin, part)]

    def lens_sums(o):
        share(o, 1 - y).wait_recv()
        m = m_ref[o]
        cm, sm = quarter_turns(m)
        values = lens[o]
        degree = 2 * h * rows + lax.broadcasted_iota(jnp.int32, values.shape, 0)
        values = jnp.where(degree >= m, values, jnp.zeros_like(values))
        flat, split = (line * circles, 2 * rows), (line, circles, csims)
        theta = jnp.dot(ltab[2 + (m & 1)].reshape(flat), values, preferred_element_type=F32)
        lpart[o, :, :, :csims] = ((sm - cm) * theta).reshape(split)
        flow = jnp.dot(ltab[m & 1].reshape(flat), values, preferred_element_type=F32)
        lpart[o, :, :, csims:] = ((cm + sm) * (m.astype(F32) * (1.0 / lmax)) * flow).reshape(split)

    def stage(t, o):
        def leftward(target, carry):
            @pl.when((target <= h) & (h < line - 1))
            def _():
                chain(0, target, o).wait_recv()
                lpart[o, target] += crecv[0, target, o].astype(F32)

            @pl.when(target < h)
            def _():
                csend[0, target, o] = lpart[o, target].astype(BF)
                chain(0, target, o).start()

            return carry

        def rightward(target, carry):
            @pl.when((target >= h) & (h > 0))
            def _():
                chain(1, target, o).wait_recv()
                lpart[o, target] += crecv[1, target, o].astype(F32)

            @pl.when(target > h)
            def _():
                csend[1, target, o] = lpart[o, target].astype(BF)
                chain(1, target, o).start()

            return carry

        @pl.when(h == line - 1 - t)
        def _():
            lax.fori_loop(0, line, leftward, 0)

        @pl.when(h == t)
        def _():
            lax.fori_loop(0, line, rightward, 0)

    def hop(s, o):
        after, before = h + s, h - s

        @pl.when(after < line)
        def _():
            along(held.at[after, o], after, o, 0).wait_recv()

            @pl.when(h > 0)
            def _():
                along(held.at[after, o], after, o, 0).start()

        @pl.when(before >= 0)
        def _():
            along(held.at[before, o], before, o, 1).wait_recv()

            @pl.when(h < line - 1)
            def _():
                along(held.at[before, o], before, o, 1).start()

        @pl.when(after < line)
        def _():
            acc[o] += product(held[after, o], after, o)

        @pl.when(before >= 0)
        def _():
            acc[o] += product(held[before, o], before, o)

    def emode_maps(o):
        cm, sm = quarter_turns(m_ref[o])
        factor = m_ref[o].astype(F32) * (1.0 / lmax)
        c0, s0, gc0, gs0 = (acc[o, 2 * k * circles : 2 * (k + 1) * circles] for k in range(4))
        a, b = cm * c0 + sm * s0, cm * s0 - sm * c0
        gc, gs = cm * gc0 + sm * gs0, cm * gs0 - sm * gc0
        maps = (
            -(pc * (gs + kappa * b) + ps * (gc + kappa * a)),
            -(pc * (gs - kappa * b) - ps * (gc - kappa * a)),
            factor * (pc * a - ps * b),
            factor * (pc * a + ps * b),
        )
        for k, value in enumerate(maps):
            at = slice(k * csims, (k + 1) * csims)
            own[o, :, at] = value[:circles]
            ysend[o, :, at] = value[circles:].astype(BF)
        across(o).start()

    def one_phase(s, outer):
        def one_order(o, carry):
            @pl.when(s < line)
            def _():
                hop(s, o)

            @pl.when(s == 1)
            def _():
                lens_sums(o)

            @pl.when(s == line - 1)
            def _():
                emode_maps(o)

            stage(s - 1, o)

            @pl.when(s == line)
            def _():
                finish(o)

            return carry

        return lax.fori_loop(0, orders, one_order, outer)

    def own_product(o, carry):
        acc[o] = product(e_ref[o], h, o)
        return carry

    lax.fori_loop(0, orders, own_product, 0)
    lax.fori_loop(1, line + 1, one_phase, 0)

    def settle(o, carry):
        across(o).wait_send()
        share(o, y).wait_send()
        for peer in peers:
            spread(o, peer, order_pos).wait_send()
            spread(o, peer, peer).wait_recv()

        def sent(block, inner):
            @pl.when((h > 0) & (block >= h))
            def _():
                along(held.at[block, o], block, o, 0).wait_send()

            @pl.when((h < line - 1) & (block <= h))
            def _():
                along(held.at[block, o], block, o, 1).wait_send()

            @pl.when(block < h)
            def _():
                chain(0, block, o).wait_send()

            @pl.when(block > h)
            def _():
                chain(1, block, o).wait_send()

            return inner

        lax.fori_loop(0, line, sent, 0)
        return carry

    lax.fori_loop(0, orders, settle, 0)
    out_ref[...] = land[...]


def pixel_kernel(orders, csims, par_ref, w_ref, m_ref, f_ref, ft_ref, out_ref):
    count = m_ref.shape[0]
    sims = csims // 2
    low = lax.broadcasted_iota(jnp.int32, (orders, csims), 1) < sims
    begin = pl.program_id(0) * count

    def halves(x, y):
        first = jnp.where(low, x, pltpu.roll(y, sims, 1))
        second = jnp.where(low, pltpu.roll(x, sims, 1), y)
        return first, second

    for c in range(count):
        qt, ut, qc, uc, dt, dc = (
            m_ref[c, :, k * csims : (k + 1) * csims].astype(F32) for k in range(6)
        )
        t_re, t_im = halves(qt, ut)
        c_re, c_im = halves(qc, uc)
        dt_re, dt_im = halves(dt, dt)
        dc_re, dc_im = halves(dc, dc)
        real = jnp.concatenate([t_re, -c_im, dt_re, -dc_im], axis=1)
        imag = jnp.concatenate([t_im, c_re, dt_im, dc_re], axis=1)
        arranged = jnp.concatenate([real, imag], axis=0).astype(BF)
        parity = par_ref[begin + c]
        pixels = jnp.dot(ft_ref[parity], arranged, preferred_element_type=F32)
        deflected = (
            pixels[:, 2 * csims : 3 * csims] * pixels[:, :csims]
            + pixels[:, 3 * csims :] * pixels[:, csims : 2 * csims]
        ).astype(BF)
        analysed = jnp.dot(f_ref[parity], deflected, preferred_element_type=F32) * w_ref[begin + c]
        gq, gu = halves(analysed[:orders], analysed[orders:])
        out_ref[c, :, :csims] = gq.astype(BF)
        out_ref[c, :, csims:] = gu.astype(BF)


def adjoint_kernel(
    lmax, circle_total, line, order_size, orders, csims,
    m_ref, r_ref, rc_ref, w_ref, grad_ref, curl_ref,
    gath, tab, acc, zs, zr, ys, yr, as_, ar,
):
    order_pos, blk, h, y, pair, peers = neighbours(order_size, line)
    degrees = grad_ref.shape[0]
    circles = gath.shape[2]
    part = w_ref.shape[1]
    amplitude = math.sqrt(2.0 / lmax)

    def back(peer, source):
        begin = pl.multiple_of(source * part, part)
        return remote(
            w_ref.at[pl.ds(peer * orders, orders)], gath.at[blk, :, pl.ds(begin, part)],
            as_.at[peer], ar.at[source], {"order": peer},
        )

    def along(line_at, way):
        block = gath.at[2 * line_at + y]
        return remote(block, block, zs.at[way, line_at], zr.at[line_at], {"blk": blk - 2 + 4 * way})

    def across(line_at, lane):
        block = gath.at[2 * line_at + lane]
        return remote(block, block, ys.at[line_at], yr.at[line_at], {"blk": pair})

    greet(order_size, line)
    for peer in peers:
        back(peer, order_pos).start()
    begin = pl.multiple_of(order_pos * part, part)
    gath[blk, :, pl.ds(begin, part), :] = w_ref[pl.ds(order_pos * orders, orders)]

    def make_table(block, carry):
        degree = blk * degrees + lax.broadcasted_iota(jnp.int32, (degrees, 1), 0)
        sine, cosine = sin_cos((2 * degree + 1) * (2 * r_ref[block] + 1), 8 * circle_total)
        tab[block, :, :circles] = (cosine * amplitude).astype(BF)
        tab[block, :, circles:] = (sine * amplitude).astype(BF)
        return carry

    lax.fori_loop(0, line // 2, make_table, 0)

    def add(block):
        ps, pc = sin_cos(2 * (2 * rc_ref[block] + 1), 8 * circle_total)
        ups, vps = [], []
        for o in range(orders):
            cm, sm = quarter_turns(m_ref[o])
            gq = gath[block, o, :, :csims].astype(F32)
            gu = gath[block, o, :, csims:].astype(F32)
            x1, y1 = pc * (gq + gu), ps * (gq - gu)
            x2, y2 = pc * (gu - gq), ps * (gu + gq)
            ups += [(cm * x1 + sm * y1).astype(BF), (cm * x2 + sm * y2).astype(BF)]
            vps += [(sm * x1 - cm * y1).astype(BF), (sm * x2 - cm * y2).astype(BF)]
        values = jnp.concatenate(
            [jnp.concatenate(ups, axis=1), jnp.concatenate(vps, axis=1)], axis=0
        )
        acc[...] += jnp.dot(tab[block], values, preferred_element_type=F32)

    for peer in peers:
        back(peer, peer).wait_recv()

    @pl.when(h > 0)
    def _():
        along(h, 0).start()

    @pl.when(h < line - 1)
    def _():
        along(h, 1).start()

    across(h, y).start()
    lax.fori_loop(line // 2, 2 * line, make_table, 0)
    acc[...] = jnp.zeros_like(acc)

    def hop(s, carry):
        after, before = h + s, h - s

        @pl.when((s > 0) & (after < line))
        def _():
            along(after, 0).wait_recv()

            @pl.when(h > 0)
            def _():
                along(after, 0).start()

            across(after, y).start()

        @pl.when((s > 0) & (before >= 0))
        def _():
            along(before, 1).wait_recv()

            @pl.when(h < line - 1)
            def _():
                along(before, 1).start()

            across(before, y).start()

        @pl.when(after < line)
        def _():
            add(2 * after + y)

        @pl.when((s > 0) & (before >= 0))
        def _():
            add(2 * before + y)

        return carry

    lax.fori_loop(0, line, hop, 0)

    def cross(s, carry):
        after, before = h + s, h - s

        @pl.when(after < line)
        def _():
            across(after, 1 - y).wait_recv()
            add(2 * after + 1 - y)

        @pl.when((s > 0) & (before >= 0))
        def _():
            across(before, 1 - y).wait_recv()
            add(2 * before + 1 - y)

        return carry

    lax.fori_loop(0, line, cross, 0)
    for peer in peers:
        back(peer, order_pos).wait_send()

    def settle(line_at, carry):
        across(line_at, y).wait_send()

        @pl.when((h > 0) & (line_at >= h))
        def _():
            along(line_at, 0).wait_send()

        @pl.when((h < line - 1) & (line_at <= h))
        def _():
            along(line_at, 1).wait_send()

        return carry

    lax.fori_loop(0, line, settle, 0)
    rows = blk * degrees + lax.broadcasted_iota(jnp.int32, (degrees, csims), 0)
    for o in range(orders):
        inside = rows >= m_ref[o]
        at = slice(o * csims, (o + 1) * csims)
        grad = acc[:, 2 * o * csims : (2 * o + 1) * csims]
        curl = acc[:, (2 * o + 1) * csims : (2 * o + 2) * csims]
        grad_ref[:, at] = jnp.where(inside, grad, 0.0).astype(BF)
        curl_ref[:, at] = jnp.where(inside, curl, 0.0).astype(BF)


def longitude_table(lmax, parity, order_list):
    full_circle = 2 * lmax
    longitude = jnp.arange(LONGS, dtype=jnp.int32)
    phase_steps = order_list[None, :, None] * (2 * longitude[None, None, :] + parity[:, None, None])
    phase_steps = jnp.mod(phase_steps, 2 * full_circle)
    angles = phase_steps.astype(jnp.float32) * (math.pi / full_circle)
    scaling = 1.0 / math.sqrt(order_list.shape[0])
    fourier = jnp.concatenate([jnp.cos(angles) * scaling, -jnp.sin(angles) * scaling], axis=1)
    return fourier.astype(BF)


def divisor(total, limit):
    return next(k for k in range(min(total, limit), 0, -1) if total % k == 0)


SMEM = pl.BlockSpec(memory_space=pltpu.SMEM)
VMEM = pl.BlockSpec(memory_space=pltpu.VMEM)
HBM = pl.BlockSpec(memory_space=pltpu.HBM)
PARAMS = pltpu.CompilerParams(vmem_limit_bytes=48 << 20)


def by_circle(order_size, blk_size, emode_coeffs, lensing_coeffs, order_values, circle_indices, circle_weights):
    degree_local, orders, csims = emode_coeffs.shape
    lmax = degree_local * blk_size
    circle_total = circle_indices.shape[0]
    order_total = order_values.shape[0]
    circles = circle_total // blk_size
    order_pos = lax.axis_index("order")
    block_pos = lax.axis_index("blk")
    my_orders = lax.dynamic_slice_in_dim(order_values, order_pos * orders, orders)
    width = orders * csims
    line = blk_size // 2
    blocks = circle_indices.reshape(blk_size, circles)
    pair_circles = jnp.concatenate(
        [
            lax.dynamic_index_in_dim(blocks, block_pos, 0, keepdims=False),
            lax.dynamic_index_in_dim(blocks, block_pos ^ 1, 0, keepdims=False),
        ]
    )
    line_circles = lax.dynamic_index_in_dim(
        circle_indices.reshape(line, 2, circles), block_pos % 2, 1, keepdims=False
    )
    fourier = longitude_table(lmax, jnp.arange(2, dtype=jnp.int32), order_values)
    fourier_t = fourier.transpose(0, 2, 1)
    part = circles // order_size
    dma = pltpu.SemaphoreType.DMA
    spread = pl.pallas_call(
        functools.partial(synth_kernel, lmax, circle_total, line, order_size, orders, csims),
        out_shape=jax.ShapeDtypeStruct((order_total, part, 6 * csims), BF),
        in_specs=[SMEM, VMEM, VMEM, VMEM, VMEM],
        out_specs=VMEM,
        scratch_shapes=[
            pltpu.VMEM((line, orders, degree_local, csims), BF),
            pltpu.VMEM((order_total, part, 6 * csims), BF),
            pltpu.VMEM((line, 8 * circles, degree_local), BF),
            pltpu.VMEM((orders, 8 * circles, csims), F32),
            pltpu.VMEM((orders, circles, 4 * csims), F32),
            pltpu.VMEM((orders, circles, 4 * csims), BF),
            pltpu.VMEM((orders, circles, 4 * csims), BF),
            pltpu.VMEM((orders, circles, 6 * csims), BF),
            pltpu.VMEM((orders, 2 * degree_local, csims), BF),
            pltpu.VMEM((4, line, circles, 2 * degree_local), BF),
            pltpu.VMEM((orders, line, circles, 2 * csims), F32),
            pltpu.VMEM((2, line, orders, circles, 2 * csims), BF),
            pltpu.VMEM((2, line, orders, circles, 2 * csims), BF),
            dma((2, line, orders)),
            dma((line, orders)),
            dma((orders,)),
            dma((orders,)),
            dma((order_size, orders)),
            dma((order_size, orders)),
            dma((orders,)),
            dma((orders,)),
            dma((2, line, orders)),
            dma((2, line, orders)),
        ],
        compiler_params=pltpu.CompilerParams(
            vmem_limit_bytes=48 << 20, collective_id=0, has_side_effects=True
        ),
        name="synth",
    )(
        my_orders,
        pair_circles[:, None],
        line_circles[:, :, None],
        emode_coeffs.transpose(1, 0, 2),
        lensing_coeffs.transpose(1, 0, 2),
    )
    spread = spread.transpose(1, 0, 2)
    begin = block_pos * circles + order_pos * part
    part_circles = lax.dynamic_slice_in_dim(circle_indices, begin, part)
    part_weights = lax.dynamic_slice_in_dim(circle_weights, begin, part)
    count = divisor(part, 8)
    weighted = pl.pallas_call(
        functools.partial(pixel_kernel, order_total, csims),
        out_shape=jax.ShapeDtypeStruct((part, order_total, 2 * csims), BF),
        grid=(part // count,),
        in_specs=[
            SMEM,
            SMEM,
            pl.BlockSpec((count, order_total, 6 * csims), lambda i: (i, 0, 0)),
            pl.BlockSpec((2, 2 * order_total, LONGS), lambda i: (0, 0, 0)),
            pl.BlockSpec((2, LONGS, 2 * order_total), lambda i: (0, 0, 0)),
        ],
        out_specs=pl.BlockSpec((count, order_total, 2 * csims), lambda i: (i, 0, 0)),
        compiler_params=PARAMS,
        name="pixels",
    )(jnp.mod(part_circles, 2), part_weights, spread, fourier, fourier_t)
    grad, curl = pl.pallas_call(
        functools.partial(adjoint_kernel, lmax, circle_total, line, order_size, orders, csims),
        out_shape=[jax.ShapeDtypeStruct((degree_local, width), BF)] * 2,
        in_specs=[SMEM, VMEM, VMEM, VMEM],
        out_specs=[VMEM, VMEM],
        scratch_shapes=[
            pltpu.VMEM((blk_size, orders, circles, 2 * csims), BF),
            pltpu.VMEM((blk_size, degree_local, 2 * circles), BF),
            pltpu.VMEM((degree_local, 2 * width), F32),
            dma((2, line)),
            dma((line,)),
            dma((line,)),
            dma((line,)),
            dma((order_size,)),
            dma((order_size,)),
        ],
        compiler_params=pltpu.CompilerParams(
            vmem_limit_bytes=48 << 20, collective_id=1, has_side_effects=True
        ),
        name="adjoint",
    )(my_orders, blocks[:, None, :], blocks[:, :, None], weighted.transpose(1, 0, 2))
    return grad.reshape(emode_coeffs.shape), curl.reshape(emode_coeffs.shape)


def turned(dims, left, right):
    return lax.dot_general(left, right, (dims, ((), ())), preferred_element_type=F32)


def realization_kernel(
    lmax, circle_total, order_size, blk_size, orders, csims, group,
    em_ref, le_ref, m_any, ci_any, cw_any, grad_ref, curl_ref,
    raw, wide, flat_in, m_ref, ci_ref, cw_ref,
    pick, out1, land1, out2, land2, tab, xs, maps, waves, waves_t, ana, pairs, wlane,
    s1, r1, s2, r2, pull,
):
    order_pos, blk = lax.axis_index("order"), lax.axis_index("blk")
    devices = order_size * blk_size
    me = order_pos * blk_size + blk
    degrees = em_ref.shape[0] // orders
    half = degrees // 2
    sims = csims // 2
    low = blk_size // 2
    span = low * half
    couples = circle_total // 2
    quarter = couples // 2
    rows = order_size * 2 * orders
    tile = 2 * orders
    full = 8 * circle_total
    width = orders * csims

    pulls = [
        pltpu.make_async_copy(src, dst, pull.at[k])
        for k, (src, dst) in enumerate(
            ((em_ref, raw.at[0]), (le_ref, raw.at[1]), (m_any, m_ref), (ci_any, ci_ref), (cw_any, cw_ref))
        )
    ]
    for copy in pulls:
        copy.start()

    late_from = blk_size - blk_size // 4
    early = blk < late_from
    early_total = order_size * late_from
    late_total = devices - early_total

    def each(begin, end, act):
        def one(k, carry):
            b = begin + lax.div(k, order_size)
            o = lax.rem(order_pos + lax.rem(k, order_size), order_size)

            @pl.when((o != order_pos) | (b != blk))
            def _():
                act(o, b)

            return carry

        lax.fori_loop(0, (end - begin) * order_size, one, 0)

    def hand(src, dst, send, recv, s, o, b):
        return pltpu.make_async_remote_copy(
            src_ref=src.at[s, o, b], dst_ref=dst.at[s, order_pos, blk],
            send_sem=send.at[s, o, b], recv_sem=recv.at[s, order_pos, blk],
            device_id={"order": o, "blk": b}, device_id_type=MESH,
        )

    def arrival(src, dst, send, recv, s, o, b):
        return pltpu.make_async_remote_copy(
            src_ref=src.at[s, o, b], dst_ref=dst.at[s, o, b],
            send_sem=send.at[s, o, b], recv_sem=recv.at[s, o, b],
            device_id={"order": o, "blk": b}, device_id_type=MESH,
        )

    first = (out1, land1, s1, r1)
    second = (out2, land2, s2, r2)

    def send_to(args, s, begin, end):
        each(begin, end, lambda o, b: hand(*args, s, o, b).start())

    def send_all(args, s):
        each(0, blk_size, lambda o, b: hand(*args, s, o, b).start())

    def await_all(args, s):
        each(0, blk_size, lambda o, b: arrival(*args, s, o, b).wait_recv())

    def sent_all(args, s):
        each(0, blk_size, lambda o, b: hand(*args, s, o, b).wait_send())

    barrier = pltpu.get_barrier_semaphore()

    def hail(begin, end):
        each(
            begin, end,
            lambda o, b: pl.semaphore_signal(
                barrier, inc=1, device_id={"order": o, "blk": b}, device_id_type=MESH
            ),
        )

    @pl.when(early)
    def _():
        hail(0, late_from)

    @pl.when(jnp.logical_not(early))
    def _():
        hail(late_from, blk_size)

    def strands():
        for o in range(orders):
            for parity in range(2):
                yield (
                    pl.ds(o + orders * parity, half, stride=2 * orders),
                    slice(parity * half, (parity + 1) * half), slice(o * csims, (o + 1) * csims),
                )

    def unpack(k):
        pulls[k].wait()
        wide[k] = raw[k].astype(F32)
        for mixed, rows_at, lanes_at in strands():
            flat_in[k, rows_at, lanes_at] = wide[k, mixed, :].astype(BF)

    def choose(s):
        row = lax.broadcasted_iota(jnp.int32, (devices * tile, 1), 0)
        within = lax.rem(row, tile)
        column = (
            lax.rem(within, orders) * csims + lax.div(within, orders) * sims + lax.div(row, tile) * group + s
        )
        lane = lax.broadcasted_iota(jnp.int32, (devices * tile, width), 1)
        choice = jnp.where(lane == column, 1.0, 0.0).astype(BF)
        pick[s] = choice

    def arrange(s):
        split = (devices, tile, degrees)
        e = turned(((1,), (1,)), pick[s], flat_in[0]).reshape(split)
        p = turned(((1,), (1,)), pick[s], flat_in[1]).reshape(split)
        both = jnp.concatenate([e, p], axis=1).astype(BF)
        out1[s] = both.reshape(order_size, blk_size, 2 * tile, degrees)
        land1[s, order_pos, blk] = out1[s, order_pos, blk]

    choose(0)
    for k in range(2):
        unpack(k)
    arrange(0)

    @pl.when(early)
    def _():
        pl.semaphore_wait(barrier, early_total - 1)
        hail(late_from, blk_size)
        send_to(first, 0, 0, late_from)

    @pl.when(jnp.logical_not(early))
    def _():
        pl.semaphore_wait(barrier, devices - 1)
        hail(0, late_from)
        send_to(first, 0, 0, blk_size)

    for s in range(1, group):
        choose(s)
        arrange(s)

    @pl.when(early)
    def _():
        pl.semaphore_wait(barrier, late_total)
        send_to(first, 0, late_from, blk_size)

    for s in range(1, group):
        send_all(first, s)

    for copy in pulls[2:]:
        copy.wait()
    amplitude = math.sqrt(2.0 / lmax)
    chunk = 64

    def make_table(i, carry):
        begin = pl.multiple_of(i * chunk, chunk)
        q = i * chunk + lax.broadcasted_iota(jnp.int32, (chunk, 1), 0)
        colat = 2 * (2 * lax.rem(q, quarter) + lax.div(q, quarter)) + 1
        step = 4 * lax.broadcasted_iota(jnp.int32, (1, half), 1)
        sb, cb = sin_cos(colat * step, full)
        k = lax.broadcasted_iota(jnp.int32, (1, 128), 1)
        start = 2 * degrees * lax.rem(k, low) + 2 * lax.div(k, low) + 1
        sa, ca = sin_cos(colat * start, full)
        sa, ca = sa * amplitude, ca * amplitude
        for n in range(2 * low):
            at = slice(n * half, (n + 1) * half)
            s0, c0 = sa[:, n : n + 1], ca[:, n : n + 1]
            tab[pl.ds(begin, chunk), at] = (c0 * cb - s0 * sb).astype(BF)
            tab[pl.ds(couples + begin, chunk), at] = (s0 * cb + c0 * sb).astype(BF)
        return carry

    lax.fori_loop(0, couples // chunk, make_table, 0)

    row = lax.broadcasted_iota(jnp.int32, (rows, 1), 0)
    slot = lax.div(row, tile) * orders + lax.rem(row, orders)
    imaginary = lax.rem(lax.div(row, orders), 2) == 1
    order_total = m_ref.shape[1]
    slots = lax.broadcasted_iota(jnp.int32, (rows, order_total), 1)
    m = jnp.sum(
        jnp.where(slots == slot, m_ref[...].astype(F32), 0.0), axis=1, keepdims=True
    ).astype(jnp.int32)
    cm, sm = quarter_turns(m)
    factor = m.astype(F32) * (1.0 / lmax)

    lane = lax.broadcasted_iota(jnp.int32, (1, circle_total), 1)
    at_couple = lax.rem(lane, couples)
    near = 2 * lax.rem(at_couple, quarter) + lax.div(at_couple, quarter)
    circle = jnp.where(lane < couples, near, circle_total - 1 - near)
    ps, pc = sin_cos(2 * (2 * circle + 1), full)

    index_t = ci_ref[...].astype(F32).T
    weight_t = cw_ref[...].T
    circle_f = circle.astype(F32)
    total = jnp.zeros((8, circle_total), F32)
    for k in range(ci_ref.shape[0]):
        for g in range(ci_ref.shape[1] // 8):
            at = slice(8 * g, 8 * g + 8)
            total += jnp.where(index_t[at, k : k + 1] == circle_f, weight_t[at, k : k + 1], 0.0)
    wlane[...] = jnp.sum(total, axis=0, keepdims=True)

    scaling = 1.0 / math.sqrt(order_total)
    turn = 2 * lmax
    longitude = lax.broadcasted_iota(jnp.int32, (1, LONGS), 1)
    for parity in range(2):
        si, co = sin_cos(m * (2 * longitude + parity), 2 * turn)
        si, co = si * scaling, co * scaling
        straight = jnp.where(imaginary, -si, co)
        crossed = jnp.where(imaginary, -co, -si)
        waves_t[parity] = straight.astype(BF)
        waves[parity, 0] = straight.T.astype(BF)
        waves[parity, 1] = crossed.T.astype(BF)

    kappa = 2.0 / (2.0 * lmax)
    within_deg = lax.broadcasted_iota(jnp.int32, (1, degrees), 1)
    within_deg = 2 * lax.rem(within_deg, half) + lax.div(within_deg, half)

    def process(s, carry):
        await_all(first, s)

        def fold(b, inner):
            deg = b * degrees + within_deg
            far = deg + low * degrees
            wd = (2 * deg + 1).astype(F32) * (1.0 / (2.0 * lmax))
            wf = (2 * far + 1).astype(F32) * (1.0 / (2.0 * lmax))
            one, two = land1[s, :, b].astype(F32), land1[s, :, b + low].astype(F32)
            for k in range(2):
                x = one[:, k * tile : (k + 1) * tile].reshape(rows, degrees)
                z = two[:, k * tile : (k + 1) * tile].reshape(rows, degrees)
                x = jnp.where(deg >= m, x, 0.0)
                z = jnp.where(far >= m, z, 0.0)
                flat, steep = (x - z).astype(BF), (wd * x - wf * z).astype(BF)
                for parity in range(2):
                    to = pl.ds(pl.multiple_of(parity * span + b * half, half), half)
                    of = slice(parity * half, (parity + 1) * half)
                    xs[2 * k * rows : (2 * k + 1) * rows, to] = flat[:, of]
                    xs[(2 * k + 1) * rows : (2 * k + 2) * rows, to] = steep[:, of]
            return inner

        lax.fori_loop(0, low, fold, 0)
        even = turned(((1,), (1,)), xs[:, :span], tab[:, :span])
        odd = turned(((1,), (1,)), xs[:, span:], tab[:, span:])
        plus, minus = even + odd, even - odd
        c_all = jnp.concatenate([plus[:, :couples], minus[:, couples:]], axis=1)
        s_all = jnp.concatenate([plus[:, couples:], minus[:, :couples]], axis=1)

        def turns(k):
            at = slice(k * rows, (k + 1) * rows)
            c0, s0 = c_all[at], s_all[at]
            return cm * c0 + sm * s0, cm * s0 - sm * c0

        a, b = turns(0)
        gc, gs = turns(1)
        la, _ = turns(2)
        _, lgs = turns(3)
        maps[0] = (-(pc * (gs + kappa * b) + ps * (gc + kappa * a))).astype(BF)
        maps[1] = (-(pc * (gs - kappa * b) - ps * (gc - kappa * a))).astype(BF)
        maps[2] = (-lgs).astype(BF)
        maps[3] = (factor * (pc * a - ps * b)).astype(BF)
        maps[4] = (factor * (pc * a + ps * b)).astype(BF)
        maps[5] = (factor * la).astype(BF)

        def pixels(n, inner):
            at = pl.ds(pl.multiple_of(n * quarter, quarter), quarter)
            parity = lax.rem(n + lax.div(n, 2), 2)
            qt, ut, dt = (
                jnp.dot(waves[parity, 0], maps[k, :, at], preferred_element_type=F32) for k in range(3)
            )
            qp, up, dp = (
                jnp.dot(waves[parity, 1], maps[k, :, at], preferred_element_type=F32) for k in range(3, 6)
            )
            dq = (dt * qt + dp * qp).astype(BF)
            du = (dt * ut + dp * up).astype(BF)
            w = wlane[:, at]
            ana[0, :, at] = (jnp.dot(waves_t[parity], dq, preferred_element_type=F32) * w).astype(BF)
            ana[1, :, at] = (jnp.dot(waves_t[parity], du, preferred_element_type=F32) * w).astype(BF)
            return inner

        lax.fori_loop(0, 4, pixels, 0)
        gq, gu = ana[0].astype(F32), ana[1].astype(F32)
        x1, y1 = pc * (gq + gu), ps * (gq - gu)
        x2, y2 = pc * (gu - gq), ps * (gu + gq)
        for k, (x, y) in enumerate(((x1, y1), (x2, y2))):
            at = slice(k * rows, (k + 1) * rows)
            up, vp = cm * x + sm * y, sm * x - cm * y
            near_u, far_u = up[:, :couples], up[:, couples:]
            near_v, far_v = vp[:, :couples], vp[:, couples:]
            pairs[0, at, :couples] = (near_u + far_v).astype(BF)
            pairs[0, at, couples:] = (near_v + far_u).astype(BF)
            pairs[1, at, :couples] = (near_u - far_v).astype(BF)
            pairs[1, at, couples:] = (near_v - far_u).astype(BF)

        def give(b, inner):
            sums = [
                jnp.dot(
                    pairs[parity],
                    tab[:, pl.ds(pl.multiple_of(parity * span + b * half, half), half)],
                    preferred_element_type=F32,
                )
                for parity in range(2)
            ]
            sums = jnp.concatenate(sums, axis=1)
            deg = b * degrees + within_deg
            split = (order_size, tile, degrees)
            grad, curl = sums[:rows], sums[rows:]

            def packed(inside, sign):
                g = jnp.where(inside, sign * grad, 0.0).reshape(split)
                c = jnp.where(inside, sign * curl, 0.0).reshape(split)
                return jnp.concatenate([g, c], axis=1).astype(BF)

            out2[s, :, b] = packed(deg >= m, 1.0)
            out2[s, :, b + low] = packed(deg + low * degrees >= m, -1.0)
            return inner

        lax.fori_loop(0, low, give, 0)
        land2[s, order_pos, blk] = out2[s, order_pos, blk]
        send_all(second, s)
        return carry

    lax.fori_loop(0, group, process, 0)

    for s in range(group):
        await_all(second, s)
        got = land2[s].astype(F32).reshape(devices, 2 * tile, degrees)
        for k, ref in enumerate((grad_ref, curl_ref)):
            z = got[:, k * tile : (k + 1) * tile].reshape(devices * tile, degrees).astype(BF)
            value = turned(((0,), (0,)), z, pick[s])
            for mixed, rows_at, lanes_at in strands():
                part = value[rows_at, lanes_at]
                if s:
                    part = part + wide[k, mixed, :]
                wide[k, mixed, :] = part
            if s == group - 1:
                ref[...] = wide[k].astype(BF)

    for s in range(group):
        sent_all(first, s)
        sent_all(second, s)


def store_kernel(grad_ref, curl_ref, grad_out, curl_out, done):
    copies = [
        pltpu.make_async_copy(src, dst, done.at[k])
        for k, (src, dst) in enumerate(((grad_ref, grad_out), (curl_ref, curl_out)))
    ]
    for copy in copies:
        copy.start()
    for copy in copies:
        copy.wait()


def by_realization(order_size, blk_size, emode_coeffs, lensing_coeffs, order_values, circle_indices, circle_weights):
    degrees, orders, csims = emode_coeffs.shape
    lmax = degrees * blk_size
    circle_total = circle_indices.shape[0]
    devices = order_size * blk_size
    group = csims // 2 // devices
    width = orders * csims
    tile = 2 * orders
    rows = order_size * tile

    dma = pltpu.SemaphoreType.DMA
    mail = pltpu.VMEM((group, order_size, blk_size, 2 * tile, degrees), BF)
    box = dma((group, order_size, blk_size))
    grad, curl = pl.pallas_call(
        functools.partial(
            realization_kernel, lmax, circle_total, order_size, blk_size, orders, csims, group
        ),
        out_shape=[jax.ShapeDtypeStruct((degrees * orders, csims), BF)] * 2,
        in_specs=[pl.BlockSpec(memory_space=pl.ANY)] * 5,
        out_specs=[VMEM, VMEM],
        scratch_shapes=[
            pltpu.VMEM((2, degrees * orders, csims), BF),
            pltpu.VMEM((2, degrees * orders, csims), F32),
            pltpu.VMEM((2, degrees, width), BF),
            pltpu.VMEM((1, order_values.shape[0]), jnp.int32),
            pltpu.VMEM((circle_total // 128, 128), jnp.int32),
            pltpu.VMEM((circle_total // 128, 128), F32),
            pltpu.VMEM((group, devices * tile, width), BF),
            mail, mail, mail, mail,
            pltpu.VMEM((circle_total, lmax // 2), BF),
            pltpu.VMEM((4 * rows, lmax // 2), BF),
            pltpu.VMEM((6, rows, circle_total), BF),
            pltpu.VMEM((2, 2, LONGS, rows), BF),
            pltpu.VMEM((2, rows, LONGS), BF),
            pltpu.VMEM((2, rows, circle_total), BF),
            pltpu.VMEM((2, 2 * rows, circle_total), BF),
            pltpu.VMEM((1, circle_total), F32),
            box, box, box, box,
            dma((5,)),
        ],
        compiler_params=pltpu.CompilerParams(
            vmem_limit_bytes=55200000, collective_id=2, has_side_effects=True
        ),
        name="remap",
    )(
        emode_coeffs.reshape(degrees * orders, csims),
        lensing_coeffs.reshape(degrees * orders, csims),
        order_values.reshape(1, -1),
        circle_indices.reshape(-1, 128),
        circle_weights.reshape(-1, 128),
    )
    grad, curl = pl.pallas_call(
        store_kernel,
        out_shape=[jax.ShapeDtypeStruct(grad.shape, BF)] * 2,
        in_specs=[VMEM, VMEM],
        out_specs=[HBM, HBM],
        scratch_shapes=[dma((2,))],
        compiler_params=pltpu.CompilerParams(vmem_limit_bytes=1 << 20),
        name="store",
    )(grad, curl)
    return grad.reshape(emode_coeffs.shape), curl.reshape(emode_coeffs.shape)


def splits_by_realization(order_size, blk_size, emode_coeffs, circle_indices):
    degrees, orders, csims = emode_coeffs.shape
    circle_total = circle_indices.shape[0]
    return (
        (csims // 2) % (order_size * blk_size) == 0
        and orders == 4
        and blk_size % 2 == 0
        and degrees % 256 == 0
        and degrees * blk_size == 4 * circle_total
        and circle_total % 512 == 0
    )


def body(order_size, blk_size, *arrays):
    if splits_by_realization(order_size, blk_size, arrays[0], arrays[3]):
        return by_realization(order_size, blk_size, *arrays)
    return by_circle(order_size, blk_size, *arrays)


def solution(mesh):
    in_specs = (P("blk", "order", None), P("blk", "order", None), P(), P(), P())
    out_specs = (P("blk", "order", None), P("blk", "order", None))
    sizes = (mesh.shape["order"], mesh.shape["blk"])
    return jax.shard_map(
        functools.partial(body, *sizes), mesh=mesh, in_specs=in_specs, out_specs=out_specs, check_vma=False
    )
```
